32 devices in a mesh: grp: 4 (over y, x), wide: 8 (over z, core).
Axes of the slice: x: 2, y: 2, z: 4, core: 2. Of those that a mesh axis runs over, the one named last changes fastest.
Arguments:
- sequences: bfloat16 [32, 128, 512], P(('grp', 'wide')), may hold values from -6 to 6
- upstream: bfloat16 [32, 128, 512], P(('grp', 'wide')), may hold values from -6 to 6
- lengths: int32 [4, 8, 1], P('grp'), may hold values from 16 to 128
- swap_table: int32 [4, 4, 1], P('grp'), may hold values from 0 to 1
- input_weight: bfloat16 [512, 2048], replicated, may hold values from -0.25 to 0.25
- output_weight: bfloat16 [512, 512], replicated, may hold values from -0.25 to 0.25
Outputs:
- layer_out: bfloat16 [32, 128, 512], P(('grp', 'wide'))
- input_grad: bfloat16 [32, 128, 512], P(('grp', 'wide'))
- input_weight_gradient: float32 [512, 2048], P('wide')
- output_weight_gradient: float32 [512, 512], P('wide')
The draws below stay inside these ranges and needn't reach their ends.
All inputs are finite; a program needn't handle non-finite values.
Results may differ from the reference program's by a relative error of at most 0.018.
Values may be sent and summed in bfloat16 or wider, within the bound.
A program may use at most 64 MiB of HBM per device.

```python
import jax
import jax.numpy as jnp
from jax import lax

HEADS = 8
HEAD_DIM = 64
D = 512
SEQ_DEV = 1
LEN = 128
SEQS = 32
N_GRP = 4
N_WIDE = 8


def with_ends(values, own_key, least, top_value):
    place = [jax.random.randint(jax.random.fold_in(own_key, axis), (), 0, length) for axis, length in enumerate(values.shape)]
    main_axis = values.shape.index(max(values.shape))
    next_to = place[:main_axis] + [(place[main_axis] + 1) % values.shape[main_axis]] + place[main_axis + 1:]
    return values.at[tuple(place)].set(least).at[tuple(next_to)].set(top_value)


def block_levels(rng, extent, pieces, low, top_value):
    factor_of = 1.0
    for position, shards_of in pieces:
        heights = jax.random.uniform(jax.random.fold_in(jax.random.fold_in(rng, 6), position), (shards_of,), jnp.float32, low / len(pieces), top_value / len(pieces))
        factor_of = factor_of * jnp.repeat(jnp.exp(heights), extent[position] // shards_of).reshape((-1,) + (1,) * (len(extent) - 1 - position))
    return factor_of


def centred(rng, shape, scale, bound, pieces=(), kind=jnp.bfloat16):
    gain = block_levels(rng, shape, pieces, -0.22, 0.18) if pieces else 1.0
    drawn = jax.random.normal(rng, shape, jnp.float32) * scale * gain
    return jnp.minimum(jnp.maximum(drawn, -bound), bound).astype(kind)


def setup_inputs(seed: int = 0) -> dict:
    key_of = jax.random.split(jax.random.key(seed), 7)
    sequences = centred(key_of[0], (SEQS, LEN, D), 1.0, 6.0, ((0, 32),))
    upstream = centred(key_of[1], (SEQS, LEN, D), 1.0, 6.0, ((0, 32),))
    lengths = with_ends(jax.random.randint(key_of[2], (N_GRP, N_WIDE, SEQ_DEV), max(1, LEN // 8), LEN + 1), jax.random.fold_in(key_of[2], 1), max(1, LEN // 8), LEN).astype(jnp.int32)
    swap_table = with_ends(jax.random.randint(key_of[3], (N_GRP, N_WIDE // 2, SEQ_DEV), 0, 2), jax.random.fold_in(key_of[3], 1), 0, 1).astype(jnp.int32)
    input_weight = centred(key_of[4], (D, 4 * D), D ** -0.5, 0.25)
    output_weight = centred(key_of[5], (D, D), D ** -0.5, 0.25)
    return {"sequences": sequences, "upstream": upstream, "lengths": lengths, "swap_table": swap_table, "input_weight": input_weight, "output_weight": output_weight}


epsilon = 1e-06

def normalize(values):
    return values * lax.rsqrt(lax.optimization_barrier(jnp.mean(values * values, axis=-1, keepdims=True)) + epsilon)

def layer_grads(rows, cotangent, lengths, input_weight, output_weight):
    slots, length_rows, width = rows.shape
    positions = jnp.arange(length_rows, dtype=jnp.int32)
    valid_rows = positions[None, :] < lengths[:, None]
    allowed = (positions[:, None] >= positions[None, :])[None, None] & valid_rows[:, None, None, :]
    input_single_precision = rows.astype(jnp.float32)
    norm_result_input = normalize(input_single_precision).astype(jnp.bfloat16)
    hidden_state = jnp.einsum('xbg,gm->xbm', norm_result_input.astype(jnp.float32), input_weight.astype(jnp.float32))

    def post(hidden_state, input_single_precision):
        activated = jax.nn.silu(hidden_state).astype(jnp.bfloat16)
        gate_part = activated[..., :width]
        value_part = activated[..., width:2 * width].reshape(slots, length_rows, HEADS, HEAD_DIM)
        query_part = activated[..., 2 * width:3 * width].reshape(slots, length_rows, HEADS, HEAD_DIM)
        key_part = activated[..., 3 * width:].reshape(slots, length_rows, HEADS, HEAD_DIM)
        scores = jnp.einsum('sqhc,skhc->shqk', query_part.astype(jnp.float32), key_part.astype(jnp.float32)) * HEAD_DIM ** (-0.5)
        weights = jnp.where(allowed, jax.nn.silu(scores), 0.0).astype(jnp.bfloat16)
        attended = jnp.einsum('shqk,skhc->sqhc', weights.astype(jnp.float32), value_part.astype(jnp.float32)).reshape(slots, length_rows, width)
        gate_applied = (gate_part * normalize(attended)).astype(jnp.bfloat16)
        layer_result = input_single_precision + jnp.einsum('xbg,gm->xbm', gate_applied.astype(jnp.float32), output_weight.astype(jnp.float32))
        return (layer_result.astype(jnp.bfloat16), gate_applied)
    layer_result, pull_back, gate_applied = jax.vjp(post, hidden_state, input_single_precision, has_aux=True)
    mask_applied = cotangent * valid_rows[..., None].astype(cotangent.dtype)
    hidden_state_gradient, direct_grad = pull_back(mask_applied)
    hidden_state_gradient = hidden_state_gradient.astype(jnp.bfloat16)
    norm_result_gradient = jnp.einsum('wmo,bo->wmb', hidden_state_gradient.astype(jnp.float32), input_weight.astype(jnp.float32))
    _, norm_back = jax.vjp(normalize, input_single_precision)
    input_grad = (direct_grad + norm_back(norm_result_gradient)[0]).astype(jnp.bfloat16)
    input_weight_gradient = jnp.einsum('uwn,uwo->no', norm_result_input.astype(jnp.float32), hidden_state_gradient.astype(jnp.float32))
    output_weight_gradient = jnp.einsum('uwn,uwo->no', gate_applied.astype(jnp.float32), mask_applied.astype(jnp.float32))
    return (layer_result, input_grad, input_weight_gradient, output_weight_gradient)

def reference(sequences, upstream, lengths, swap_table, input_weight, output_weight):
    group_rows = sequences.reshape(N_GRP, N_WIDE * SEQ_DEV, LEN, D)
    group_cts = upstream.reshape(N_GRP, N_WIDE * SEQ_DEV, LEN, D)
    group_lens = lengths.reshape(N_GRP, N_WIDE * SEQ_DEV).astype(jnp.int32)

    def step(carry, item):
        rows, cotangent, lens = item
        layer_result, input_grad, input_weight_gradient, output_weight_gradient = layer_grads(rows, cotangent, lens, input_weight, output_weight)
        return ((carry[0] + input_weight_gradient, carry[1] + output_weight_gradient), (layer_result, input_grad))
    start = (jnp.zeros((D, 4 * D), jnp.float32), jnp.zeros((D, D), jnp.float32))
    totals, results = lax.scan(step, start, (group_rows, group_cts, group_lens))
    outputs = results[0].reshape(N_GRP, N_WIDE, SEQ_DEV, LEN, D)
    partner = jnp.roll(outputs, N_WIDE // 2, axis=1)
    swap_flags = jnp.concatenate([swap_table, swap_table], axis=1)
    layer_out = jnp.where((swap_flags == 1)[..., None, None], partner, outputs).reshape(SEQS, LEN, D)
    input_grad = results[1].reshape(SEQS, LEN, D)
    grad_scale = (SEQS * LEN) ** (-0.5)
    return (layer_out, input_grad, totals[0] * grad_scale, totals[1] * grad_scale)
```

```python
import functools
import math

import jax
import jax.numpy as jnp
from jax import lax
from jax.experimental import pallas as pl
from jax.experimental.pallas import tpu as pltpu
from jax.sharding import PartitionSpec as P

HEADS = 8
HEAD_DIM = 64
EPSILON = 1e-06
MODES = {"out0": "z0,z1,g01,G", "out1": "z0,z1,g01,G"}
PARTS = {"gate": 0, "value": 1, "query": 0, "key": 1}
PART_Z = {"gate": "z01", "value": "z01", "query": "z01", "key": "z01"}
DRAIN = ("gate", "value", "out0", "out1", "query", "key")
LIMIT = 67043328 - 1024 * 1024
MESH = pl.DeviceIdType.MESH
F32 = jnp.float32
BF16 = jnp.bfloat16


def dot(a, b, ca=1, cb=0):
    return lax.dot_general(a, b, (((ca,), (cb,)), ((), ())), preferred_element_type=F32)


def silu_and_slope(h):
    s = jax.nn.sigmoid(h)
    return h * s, s * (1.0 + h * (1.0 - s))


def stack_heads(a, low):
    zero = jnp.zeros_like(a)
    return jnp.concatenate([jnp.where(low, a, zero), jnp.where(low, zero, a)], axis=0)


def side_by_side(a):
    half = a.shape[0] // 2
    return jnp.concatenate([a[:half], a[half:]], axis=1)


def bits_of(n):
    return n.bit_length() - 1


class Plan:
    def __init__(self, groups, shards, length, width):
        self.groups, self.shards, self.length, self.width = groups, shards, length, width
        self.chips = shards // 2
        self.share = width // shards
        self.unit = min(16, self.share)
        self.pieces = min(self.share // self.unit, groups)
        self.unit = self.share // self.pieces
        self.units = self.pieces * self.chips
        self.grp_bits = bits_of(groups)
        self.z_bits = bits_of(self.chips)
        self.q_bits = bits_of(self.pieces)
        pair = 2 * HEAD_DIM
        self.pairs = width // pair
        half = width // 2
        self.chunks = [("out%d" % i, half) for i in range(2)]
        self.chunks += [("gate%d" % i, half) for i in range(2)]
        self.chunks += [("pair%d" % p, 3 * pair) for p in range(self.pairs)]

    def stages(self, name):
        g_bits = [("g", b) for b in range(self.grp_bits)]
        z_bits = [("z", b) for b in range(self.z_bits)]
        if name not in MODES or self.q_bits != 2 or self.grp_bits != 2 or self.z_bits != 2:
            halve, rest = g_bits[: self.q_bits], g_bits[self.q_bits :]
            found = [("split", [b]) for b in halve + z_bits] + [("add", [b]) for b in rest]
            return found + ([("gather", halve)] if halve else [])
        found, halved = [], []
        for word in MODES[name].split(","):
            kind = {"g": "split", "z": "split", "a": "add", "G": "gather"}[word[0]]
            bits = [("z" if word[0] == "z" else "g", int(b)) for b in word[1:]]
            if word[0] == "g":
                halved += bits
            found.append((kind, halved if kind == "gather" else bits))
        return found

    def unit_order(self, name):
        bits = [b for kind, bits in self.stages(name) if kind == "split" for b in bits]
        whole = [("g", b) for b in range(self.q_bits) if ("g", b) not in bits]
        bits = bits + whole
        order = []
        for u in range(self.units):
            z = q = 0
            for i, (axis, b) in enumerate(bits):
                bit = (u >> (len(bits) - 1 - i)) % 2
                if axis == "z":
                    z += bit << b
                else:
                    q = q * 2 + bit
            order.append(z * self.pieces + q)
        return order

    def scratch_of(self, name, columns):
        shapes, units = [(self.units, self.unit, columns)], self.units
        for kind, bits in self.stages(name):
            if kind == "split":
                units >>= len(bits)
            if kind != "gather":
                shapes.append(((2 ** len(bits) - 1) * units, self.unit, columns))
                shapes.append((units, self.unit, columns))
            else:
                shapes.append((self.pieces, self.unit, columns))
        return shapes

    def copies(self):
        n = 5 + self.pairs
        for name, _ in self.chunks:
            for kind, bits in self.stages(name):
                n += 2 ** len(bits) - 1
        return n

    def masks(self):
        found = []
        for name, _ in self.chunks:
            for kind, bits in self.stages(name):
                for flipped in flips(bits):
                    if sorted(flipped) not in found:
                        found.append(sorted(flipped))
        top = [("z", self.z_bits - 1)]
        return found if top in found else found + [top]


def flips(bits):
    return [
        [b for i, b in enumerate(bits) if (m >> i) % 2] for m in range(1, 2 ** len(bits))
    ]


class Links:
    def __init__(self, plan, send_sem, recv_sem):
        self.send_sem, self.recv_sem, self.count, self.open = send_sem, recv_sem, 0, []
        self.g, self.w = lax.axis_index("grp"), lax.axis_index("wide")
        self.core = lax.rem(self.w, 2)
        self.z = lax.div(self.w, 2)

    def bit(self, which):
        axis, b = which
        if axis == "c":
            return self.core
        return lax.rem(lax.div(self.g if axis == "g" else self.z, 1 << b), 2)

    def partner(self, flipped):
        g, w = self.g, self.w
        for axis, b in flipped:
            step = (1 << b) * (1 - 2 * self.bit((axis, b)))
            if axis == "g":
                g = g + step
            else:
                w = w + (step if axis == "c" else 2 * step)
        return (g, w)

    def place(self, bits, flipped=()):
        at = 0
        for which in bits:
            bit = self.bit(which)
            at = at * 2 + (1 - bit if which in flipped else bit)
        return at

    def sibling(self):
        return (self.g, self.w + 1 - 2 * self.core)

    def send(self, source, target, device):
        i = self.count
        self.count += 1
        copy = pltpu.make_async_remote_copy(
            src_ref=source,
            dst_ref=target,
            send_sem=self.send_sem.at[i],
            recv_sem=self.recv_sem.at[i],
            device_id=device,
            device_id_type=MESH,
        )
        copy.start()
        self.open.append(copy)
        return copy


class Chunk:
    def __init__(self, plan, links, spec, refs, write):
        name, self.columns = spec
        self.plan, self.links, self.write = plan, links, write
        self.stages, self.order = plan.stages(name), plan.unit_order(name)
        refs = list(refs)
        self.now, self.rest = refs[0], refs[1:]
        self.units, self.step, self.copies = plan.units, 0, []

    def begin(self, lhs, rhs):
        u = self.plan.unit
        lhs = jnp.concatenate([lhs[i * u : (i + 1) * u] for i in self.order], axis=0)
        value = dot(lhs, rhs).astype(BF16)
        self.now[...] = value.reshape(self.now.shape)
        self.launch()

    def launch(self):
        kind, bits = self.stages[self.step]
        links, self.copies = self.links, []
        if kind == "gather":
            own = self.rest[0].at[pl.ds(links.place(bits), 1)]
            own[...] = self.now[...]
        for i, flipped in enumerate(flips(bits)):
            if kind == "split":
                size = self.units >> len(bits)
                source = self.now.at[pl.ds(links.place(bits, flipped) * size, size)]
                target = self.rest[0].at[pl.ds(i * size, size)]
            elif kind == "add":
                source, target = self.now, self.rest[0].at[pl.ds(i * self.units, self.units)]
            else:
                source, target = own, own
            self.copies.append(links.send(source, target, links.partner(flipped)))

    def advance(self):
        kind, bits = self.stages[self.step]
        for copy in self.copies:
            copy.wait_recv()
        if kind != "gather":
            if kind == "split":
                self.units >>= len(bits)
            size = self.units
            mine = self.links.place(bits) if kind == "split" else 0
            total = self.now[pl.ds(mine * size, size)].astype(F32)
            arrived, result = self.rest[:2]
            self.rest = self.rest[2:]
            for i in range(len(self.copies)):
                total += arrived[i * size : (i + 1) * size].astype(F32)
            result[...] = total.astype(BF16)
            self.now = result
        else:
            self.now = self.rest[0]
        self.step += 1
        if self.step < len(self.stages):
            self.launch()
            return False
        self.write(self.now[...].astype(F32).reshape(self.plan.share, self.columns))
        return True


CORE = ("c", 0)


class QuadPlan(Plan):
    def __init__(self, *sizes):
        super().__init__(*sizes)
        self.chunks = self.chunks[:2]
        self.block = self.width // 4
        self.piece = self.share // 2

    @staticmethod
    def fits(groups, shards, length, width):
        return groups == 4 and shards == 8 and width % 512 == 0 and length % 128 == 0

    def quad(self, name):
        return [("g", PARTS[name]), CORE]

    def part_stages(self, name):
        across = ("g", 1 - PARTS[name])
        words = [[("z", int(b)) for b in word[1:]] for word in PART_Z[name].split()]
        return [("split", [across])] + [("split", bits) for bits in words] + [
            ("spread", [across] + self.quad(name))
        ]

    def rows_of_units(self):
        rows = []
        for half in range(2):
            for at in range(self.chips):
                z = sum(((at >> (self.z_bits - 1 - b)) % 2) << b for b in range(self.z_bits))
                for core in range(2):
                    rows.append((2 * z + core) * self.share + half * self.piece)
        return rows

    def part_scratch(self, name):
        units = 4 * self.chips
        shapes = [(units, self.piece, self.block)]
        for kind, bits in self.part_stages(name):
            if kind == "split":
                units >>= len(bits)
                shapes.append(((2 ** len(bits) - 1) * units, self.piece, self.block))
                shapes.append((units, self.piece, self.block))
            else:
                shapes.append((8, self.piece, self.block))
        return shapes

    def copies(self):
        n = super().copies() - 5 - self.pairs + 8 + 3 * len(PARTS)
        for name in PARTS:
            n += sum(2 ** len(bits) - 1 for _, bits in self.part_stages(name))
        return n

    def masks(self):
        found = super().masks()
        for name in PARTS:
            for _, bits in self.part_stages(name):
                for flipped in flips(bits):
                    if sorted(flipped) not in found:
                        found.append(sorted(flipped))
        return [m for m in found if m != [CORE]]


class Part(Chunk):
    def __init__(self, plan, links, name, refs, write):
        self.plan, self.links, self.write, self.name = plan, links, write, name
        self.columns, self.stages = plan.block, plan.part_stages(name)
        self.now, self.rest = refs[0], list(refs[1:])
        self.units, self.step, self.copies = 4 * plan.chips, 0, []

    def begin(self, lhs, rhs):
        self.now[...] = dot(lhs, rhs).astype(BF16).reshape(self.now.shape)
        self.launch()

    def launch(self):
        kind, bits = self.stages[self.step]
        if kind != "spread":
            return super().launch()
        links, self.copies, all_of = self.links, [], self.rest[0]
        own = all_of.at[pl.ds(links.place(bits), 1)]
        own[...] = self.now[pl.ds(links.core, 1)]
        for flipped in flips(bits):
            core = 1 - links.core if CORE in flipped else links.core
            source = self.now.at[pl.ds(core, 1)]
            self.copies.append(links.send(source, own, links.partner(flipped)))

    def advance(self):
        if self.stages[self.step][0] != "spread":
            return super().advance()
        for copy in self.copies:
            copy.wait_recv()
        self.write(self.rest[0])
        return True


def quad_kernel(plan, scale, *refs):
    (lengths_hbm, swaps_hbm, x_hbm, up_hbm, win_hbm, wout_hbm, out_ref, dx_ref, diw_ref, dow_ref) = refs[:10]
    (win, wout, act, slope, weights, wslope, nt, gt, gt_peer, masked, masked_peer,
     blocks, held, home, arrived) = refs[10:25]
    lengths, swaps, x_ref, up_ref, load_sem, send_sem, recv_sem = refs[25:32]
    refs = list(refs[32:])
    length, width, block = plan.length, plan.width, plan.block
    pair, pairs = 2 * HEAD_DIM, plan.pairs
    links = Links(plan, send_sem, recv_sem)
    names = list(PARTS)

    barrier = pltpu.get_barrier_semaphore()
    friends = [links.sibling()]
    friends += [links.partner(flipped) for flipped in plan.masks()]
    for friend in friends:
        pl.semaphore_signal(barrier, inc=1, device_id=friend, device_id_type=MESH)
    moves = [(x_hbm, x_ref), (lengths_hbm, lengths), (up_hbm, up_ref), (swaps_hbm, swaps)]
    for j in range(4):
        columns = pl.ds(j * width, width)
        moves.append((win_hbm.at[:, columns], win.at[:, columns]))
    moves.append((wout_hbm, wout))
    loads = [pltpu.make_async_copy(a, b, load_sem.at[i]) for i, (a, b) in enumerate(moves)]
    for load in loads:
        load.start()
    for load in loads[:4]:
        load.wait()
    loads = loads[4:]

    live_count = lengths[0, links.w]
    flag = swaps[0, lax.rem(links.w, plan.shards // 2)]
    low = lax.broadcasted_iota(jnp.int32, (length, pair), 1) < HEAD_DIM
    query_at = lax.broadcasted_iota(jnp.int32, (length, length), 0)
    key_at = lax.broadcasted_iota(jnp.int32, (length, length), 1)
    allowed = (query_at >= key_at) & (key_at < live_count)
    allowed = jnp.concatenate([allowed, allowed], axis=0)

    x = x_ref[0].astype(F32)
    x_scale = lax.rsqrt(jnp.mean(x * x, axis=-1, keepdims=True) + EPSILON)
    normed = (x * x_scale).astype(BF16)
    across = (x * x_scale).astype(BF16).astype(F32).T
    piece = plan.piece
    for i, row in enumerate(plan.rows_of_units()):
        nt[0, i * piece : (i + 1) * piece] = across[row : row + piece].astype(BF16)
    row_at = lax.broadcasted_iota(jnp.int32, (length, width), 0)
    masked[...] = jnp.where(row_at < live_count, up_ref[0].astype(F32), 0.0).astype(BF16)
    pl.semaphore_wait(barrier, len(friends))
    nt_copies = {}
    for slot, flipped in ((2, [("g", 0)]), (4, [("g", 1)]), (1, [CORE])):
        nt_copies[slot] = links.send(nt.at[0], nt.at[slot], links.partner(flipped))
    masked_copy = links.send(masked, masked_peer, links.sibling())
    for j in range(4):
        loads[j].wait()
        columns = slice(j * width, (j + 1) * width)
        a, s = silu_and_slope(dot(normed, win[:, columns]))
        act[:, columns] = a.astype(BF16)
        slope[:, columns] = s

    def part(j, p):
        start = j * width + p * pair
        return act[:, start : start + pair]

    attended = []
    for p in range(pairs):
        scores = dot(stack_heads(part(2, p), low), part(3, p), 1, 1) * HEAD_DIM ** (-0.5)
        a, s = silu_and_slope(scores)
        a = jnp.where(allowed, a, 0.0).astype(BF16)
        weights[p] = a
        wslope[p] = jnp.where(allowed, s, 0.0) * HEAD_DIM ** (-0.5)
        attended.append(dot(side_by_side(a), stack_heads(part(1, p), low)))
    attended = jnp.concatenate(attended, axis=1)
    att_scale = lax.rsqrt(jnp.mean(attended * attended, axis=-1, keepdims=True) + EPSILON)
    gate = act[:, :width].astype(F32)
    att_normed = attended * att_scale
    gated = (gate * att_normed).astype(BF16)
    turned = gated.astype(F32).T
    for w in range(plan.shards):
        core, z = w % 2, w // 2
        for q in range(plan.pieces):
            row = w * plan.share + q * plan.unit
            gt[core, z * plan.pieces + q] = turned[row : row + plan.unit].astype(BF16)
    gt_copy = links.send(gt.at[1 - links.core], gt_peer, links.sibling())
    loads[4].wait()
    home[...] = (x + dot(gated, wout[...])).astype(BF16)
    home_copy = links.send(home, arrived, links.partner([("z", plan.z_bits - 1)]))

    gated_grad = dot(masked[...], wout[...], 1, 1).astype(BF16).astype(F32)
    gate_grad = (gated_grad * att_normed).astype(BF16).astype(F32)
    hg = (gate_grad * slope[:, :width]).astype(BF16)

    held_copies = {}

    def offer(name):
        j, quad = names.index(name), plan.quad(name)
        held[j, 0:1] = blocks[j, pl.ds(links.place(quad), 1)]
        copies = []
        for i, flipped in enumerate(flips(quad)):
            source = blocks.at[j, pl.ds(links.place(quad, flipped), 1)]
            copies.append(links.send(source, held.at[j, pl.ds(i + 1, 1)], links.partner(flipped)))
        held_copies[name] = copies

    for b in range(4):
        blocks[0, b] = hg[:, b * block : (b + 1) * block]
    offer("gate")
    norm_grad = gated_grad * gate
    along = jnp.mean(norm_grad * attended, axis=-1, keepdims=True)
    att_grad = (att_scale * norm_grad - attended * (att_scale * att_scale * att_scale * along)).astype(BF16)
    both_heads = [stack_heads(att_grad[:, p * pair : (p + 1) * pair], low) for p in range(pairs)]

    def put(j, p, grad):
        start = j * width + p * pair
        grad = (grad.astype(BF16).astype(F32) * slope[:, start : start + pair]).astype(BF16)
        blocks[j, p] = grad

    for p in range(pairs):
        put(1, p, dot(weights[p], both_heads[p], 0, 0))
    offer("value")

    chunks, flight, lines = {}, [], plan.piece

    def out_writer(i):
        half = width // 2

        def write(values):
            dow_ref[:, i * half : (i + 1) * half] = values * scale

        return write

    def part_writer(name):
        j = names.index(name)

        def write(ref):
            for m in range(8):
                row, column = (m // 4) * lines, j * width + (m % 4) * block
                diw_ref[row : row + lines, column : column + block] = ref[m].astype(F32) * scale

        return write

    for i, spec in enumerate(plan.chunks):
        n = len(plan.scratch_of(*spec))
        chunks[spec[0]] = Chunk(plan, links, spec, refs[:n], out_writer(i))
        refs = refs[n:]
    for name in names:
        n = len(plan.part_scratch(name))
        chunks[name] = Part(plan, links, name, refs[:n], part_writer(name))
        refs = refs[n:]

    masked_copy.wait_recv()
    gt_copy.wait_recv()
    mine = gt[pl.ds(links.core, 1)].reshape(width // 2, length)
    lhs = jnp.concatenate([mine, gt_peer[...].reshape(width // 2, length)], axis=1)
    for i in range(2):
        columns = slice(i * (width // 2), (i + 1) * (width // 2))
        chunks["out%d" % i].begin(lhs, jnp.concatenate([masked[:, columns], masked_peer[:, columns]], axis=0))
        flight.append("out%d" % i)

    score_grads = []
    for p in range(pairs):
        weight_grad = dot(both_heads[p], part(1, p), 1, 1).astype(BF16).astype(F32)
        score_grads.append((weight_grad * wslope[p]).astype(BF16))
        put(2, p, dot(side_by_side(score_grads[p]), stack_heads(part(3, p), low)))
    offer("query")
    for p in range(pairs):
        put(3, p, dot(score_grads[p], stack_heads(part(2, p), low), 0, 0))
    offer("key")

    for slot in (2, 4):
        nt_copies[slot].wait_recv()
        nt_copies[slot + 1] = links.send(nt.at[slot], nt.at[slot + 1], links.sibling())

    back = 0.0
    for j in range(4):
        grads = jnp.concatenate([blocks[j, b] for b in range(4)], axis=1)
        back += dot(grads, win[:, j * width : (j + 1) * width], 1, 1)
    along = jnp.mean(back * x, axis=-1, keepdims=True)
    dx = x_scale * back - x * (x_scale * x_scale * x_scale * along)
    dx_ref[0] = (masked[...].astype(F32) + dx).astype(BF16)

    waited = []

    def begin(name):
        slots = [0, 1, 2, 3] if PARTS[name] == 0 else [0, 1, 4, 5]
        for slot in slots[1:]:
            if slot % 2 and slot not in waited:
                waited.append(slot)
                nt_copies[slot].wait_recv()
        for copy in held_copies[name]:
            copy.wait_recv()
        order = [slots[0], slots[2], slots[1], slots[3]]
        lhs = jnp.concatenate([nt[slot] for slot in order], axis=1)
        chunks[name].begin(lhs, held[names.index(name)].reshape(4 * length, block))

    started = []

    def step(name):
        if name in PARTS and name not in started:
            started.append(name)
            begin(name)
            flight.append(name)
            return
        flight.remove(name)
        if not chunks[name].advance():
            flight.append(name)

    for name in DRAIN:
        step(name)
    for name in names:
        if name not in started:
            step(name)
    while flight:
        step(flight[0])
    home_copy.wait_recv()
    out_ref[0] = jnp.where(flag == 1, arrived[...].astype(F32), home[...].astype(F32)).astype(BF16)
    for copy in links.open:
        copy.wait_send()


def kernel(plan, scale, *refs):
    (lengths_hbm, swaps_hbm, x_hbm, up_hbm, win_hbm, wout_hbm, out_ref, dx_ref, diw_ref, dow_ref) = refs[:10]
    (win, wout, act, slope, weights, wslope, nt, nt_peer, gt, gt_peer, masked, masked_peer,
     hg_gate, hg_gate_peer, hg_pair, hg_pair_peer, home, arrived) = refs[10:28]
    lengths, swaps, x_ref, up_ref, load_sem, send_sem, recv_sem = refs[28:35]
    refs = list(refs[35:])
    length, width = plan.length, plan.width
    pair, pairs = 2 * HEAD_DIM, plan.pairs
    links = Links(plan, send_sem, recv_sem)

    barrier = pltpu.get_barrier_semaphore()
    friends = [links.sibling()]
    friends += [links.partner(flipped) for flipped in plan.masks()]
    for friend in friends:
        pl.semaphore_signal(barrier, inc=1, device_id=friend, device_id_type=MESH)
    moves = [(x_hbm, x_ref), (lengths_hbm, lengths), (up_hbm, up_ref), (swaps_hbm, swaps)]
    for j in range(4):
        columns = pl.ds(j * width, width)
        moves.append((win_hbm.at[:, columns], win.at[:, columns]))
    moves.append((wout_hbm, wout))
    loads = [pltpu.make_async_copy(a, b, load_sem.at[i]) for i, (a, b) in enumerate(moves)]
    for load in loads:
        load.start()
    for load in loads[:4]:
        load.wait()
    loads = loads[4:]

    live_count = lengths[0, links.w]
    flag = swaps[0, lax.rem(links.w, plan.shards // 2)]
    low = lax.broadcasted_iota(jnp.int32, (length, pair), 1) < HEAD_DIM
    query_at = lax.broadcasted_iota(jnp.int32, (length, length), 0)
    key_at = lax.broadcasted_iota(jnp.int32, (length, length), 1)
    allowed = (query_at >= key_at) & (key_at < live_count)
    allowed = jnp.concatenate([allowed, allowed], axis=0)

    def split_rows(values, target):
        across = values.astype(F32).T
        for w in range(plan.shards):
            core, z = w % 2, w // 2
            for q in range(plan.pieces):
                row = w * plan.share + q * plan.unit
                target[core, z * plan.pieces + q] = across[row : row + plan.unit].astype(BF16)

    def both(own, peer):
        mine = own[pl.ds(links.core, 1)].reshape(width // 2, length)
        return jnp.concatenate([mine, peer[...].reshape(width // 2, length)], axis=1)

    x = x_ref[0].astype(F32)
    x_scale = lax.rsqrt(jnp.mean(x * x, axis=-1, keepdims=True) + EPSILON)
    normed = (x * x_scale).astype(BF16)
    row_at = lax.broadcasted_iota(jnp.int32, (length, width), 0)
    masked[...] = jnp.where(row_at < live_count, up_ref[0].astype(F32), 0.0).astype(BF16)
    split_rows(normed, nt)
    pl.semaphore_wait(barrier, len(friends))
    masked_copy = links.send(masked, masked_peer, links.sibling())
    nt_copy = links.send(nt.at[1 - links.core], nt_peer, links.sibling())
    for j in range(4):
        loads[j].wait()
        columns = slice(j * width, (j + 1) * width)
        a, s = silu_and_slope(dot(normed, win[:, columns]))
        act[:, columns] = a.astype(BF16)
        slope[:, columns] = s

    def part(j, p):
        start = j * width + p * pair
        return act[:, start : start + pair]

    attended = []
    for p in range(pairs):
        scores = dot(stack_heads(part(2, p), low), part(3, p), 1, 1) * HEAD_DIM ** (-0.5)
        a, s = silu_and_slope(scores)
        a = jnp.where(allowed, a, 0.0).astype(BF16)
        weights[p] = a
        wslope[p] = jnp.where(allowed, s, 0.0) * HEAD_DIM ** (-0.5)
        attended.append(dot(side_by_side(a), stack_heads(part(1, p), low)))
    attended = jnp.concatenate(attended, axis=1)
    att_scale = lax.rsqrt(jnp.mean(attended * attended, axis=-1, keepdims=True) + EPSILON)
    gate = act[:, :width].astype(F32)
    att_normed = attended * att_scale
    gated = (gate * att_normed).astype(BF16)
    split_rows(gated, gt)
    gt_copy = links.send(gt.at[1 - links.core], gt_peer, links.sibling())
    loads[4].wait()
    home[...] = (x + dot(gated, wout[...])).astype(BF16)
    home_copy = links.send(home, arrived, links.partner([("z", plan.z_bits - 1)]))

    gated_grad = dot(masked[...], wout[...], 1, 1).astype(BF16).astype(F32)
    gate_grad = (gated_grad * att_normed).astype(BF16).astype(F32)
    hg_gate[...] = (gate_grad * slope[:, :width]).astype(BF16)
    hg_gate_copy = links.send(hg_gate, hg_gate_peer, links.sibling())
    norm_grad = gated_grad * gate
    along = jnp.mean(norm_grad * attended, axis=-1, keepdims=True)
    att_grad = (att_scale * norm_grad - attended * (att_scale * att_scale * att_scale * along)).astype(BF16)

    chunks, flight = {}, []

    def writer(name):
        kind, i = name.rstrip("0123456789"), int(name[-1])
        half = width // 2

        def write(values):
            values = values * scale
            if kind == "out":
                dow_ref[:, i * half : (i + 1) * half] = values
            elif kind == "gate":
                diw_ref[:, i * half : (i + 1) * half] = values
            else:
                for j in range(3):
                    start = (j + 1) * width + i * pair
                    diw_ref[:, start : start + pair] = values[:, j * pair : (j + 1) * pair]

        return write

    for spec in plan.chunks:
        n = len(plan.scratch_of(*spec))
        chunks[spec[0]] = Chunk(plan, links, spec, refs[:n], writer(spec[0]))
        refs = refs[n:]

    def begin(name, lhs, rhs):
        chunks[name].begin(lhs, rhs)
        flight.append(chunks[name])

    def advance(count):
        for _ in range(min(count, len(flight))):
            chunk = flight.pop(0)
            if not chunk.advance():
                flight.append(chunk)

    masked_copy.wait_recv()
    gt_copy.wait_recv()
    lhs = both(gt, gt_peer)
    for i in range(2):
        columns = slice(i * (width // 2), (i + 1) * (width // 2))
        begin("out%d" % i, lhs, jnp.concatenate([masked[:, columns], masked_peer[:, columns]], axis=0))

    pair_copies = []

    def pair_backward(p):
        q, k, v = part(2, p), part(3, p), part(1, p)
        q2 = stack_heads(q, low)
        da2 = stack_heads(att_grad[:, p * pair : (p + 1) * pair], low)
        weight_grad = dot(da2, v, 1, 1).astype(BF16).astype(F32)
        score_grad = (weight_grad * wslope[p]).astype(BF16)
        dv = dot(weights[p], da2, 0, 0)
        dq = dot(side_by_side(score_grad), stack_heads(k, low))
        dk = dot(score_grad, q2, 0, 0)
        for j, grad in enumerate((dv, dq, dk)):
            start = (j + 1) * width + p * pair
            grad = grad.astype(BF16).astype(F32) * slope[:, start : start + pair]
            hg_pair[p, :, j * pair : (j + 1) * pair] = grad.astype(BF16)
        pair_copies.append(links.send(hg_pair.at[p], hg_pair_peer.at[p], links.sibling()))

    def begin_pair(p):
        pair_copies[p].wait_recv()
        begin("pair%d" % p, lhs_in, jnp.concatenate([hg_pair[p], hg_pair_peer[p]], axis=0))

    pair_backward(0)
    hg_gate_copy.wait_recv()
    nt_copy.wait_recv()
    lhs_in = both(nt, nt_peer)
    for i in range(2):
        columns = slice(i * (width // 2), (i + 1) * (width // 2))
        begin("gate%d" % i, lhs_in, jnp.concatenate([hg_gate[:, columns], hg_gate_peer[:, columns]], axis=0))
    for p in range(1, pairs):
        pair_backward(p)
        begin_pair(p - 1)

    back = dot(hg_gate[...], win[:, :width], 1, 1)
    for p in range(pairs):
        if p == 1:
            begin_pair(pairs - 1)
        for j in range(3):
            start = (j + 1) * width + p * pair
            back += dot(hg_pair[p, :, j * pair : (j + 1) * pair], win[:, start : start + pair], 1, 1)
    along = jnp.mean(back * x, axis=-1, keepdims=True)
    dx = x_scale * back - x * (x_scale * x_scale * x_scale * along)
    dx_ref[0] = (masked[...].astype(F32) + dx).astype(BF16)

    while flight:
        advance(1)
    home_copy.wait_recv()
    out_ref[0] = jnp.where(flag == 1, arrived[...].astype(F32), home[...].astype(F32)).astype(BF16)
    for copy in links.open:
        copy.wait_send()


def store_kernel(*refs):
    sems = refs[8]
    copies = [pltpu.make_async_copy(refs[i], refs[4 + i], sems.at[i]) for i in range(4)]
    for copy in copies:
        copy.start()
    for copy in copies:
        copy.wait()


def body(plan, sequences, upstream, lengths, swap_table, input_weight, output_weight):
    length, width = plan.length, plan.width
    scale = 1.0 / math.sqrt(length * plan.shards * plan.groups)
    rows = plan.units, plan.unit, length
    pair, pairs = 2 * HEAD_DIM, plan.pairs
    vmem = lambda *shape: pltpu.VMEM(shape, BF16)
    quad = isinstance(plan, QuadPlan)
    if quad:
        exchanged = [
            vmem(6, width, length),
            vmem(2, *rows),
            vmem(*rows),
            vmem(length, width),
            vmem(length, width),
            vmem(4, 4, length, plan.block),
            vmem(4, 4, length, plan.block),
        ]
    else:
        exchanged = [
            vmem(2, *rows),
            vmem(*rows),
            vmem(2, *rows),
            vmem(*rows),
            vmem(length, width),
            vmem(length, width),
            vmem(length, width),
            vmem(length, width),
            vmem(pairs, length, 3 * pair),
            vmem(pairs, length, 3 * pair),
        ]
    scratch = [
        vmem(width, 4 * width),
        vmem(width, width),
        vmem(length, 4 * width),
        pltpu.VMEM((length, 4 * width), F32),
        vmem(pairs, 2 * length, length),
        pltpu.VMEM((pairs, 2 * length, length), F32),
        *exchanged,
        vmem(length, width),
        vmem(length, width),
        pltpu.SMEM((1, plan.shards), jnp.int32),
        pltpu.SMEM((1, plan.shards // 2), jnp.int32),
        vmem(1, length, width),
        vmem(1, length, width),
        pltpu.SemaphoreType.DMA((9,)),
        pltpu.SemaphoreType.DMA((plan.copies(),)),
        pltpu.SemaphoreType.DMA((plan.copies(),)),
    ]
    for spec in plan.chunks:
        scratch += [vmem(*shape) for shape in plan.scratch_of(*spec)]
    for name in PARTS if quad else ():
        scratch += [vmem(*shape) for shape in plan.part_scratch(name)]
    in_vmem = pl.BlockSpec(memory_space=pltpu.VMEM)
    in_hbm = pl.BlockSpec(memory_space=pltpu.HBM)
    results = pl.pallas_call(
        functools.partial(quad_kernel if quad else kernel, plan, scale),
        out_shape=(
            pltpu.VMEM(sequences.shape, BF16),
            pltpu.VMEM(sequences.shape, BF16),
            pltpu.VMEM((plan.share, 4 * width), F32),
            pltpu.VMEM((plan.share, width), F32),
        ),
        in_specs=[in_hbm] * 6,
        out_specs=(in_vmem,) * 4,
        scratch_shapes=scratch,
        compiler_params=pltpu.CompilerParams(
            collective_id=0, has_side_effects=True, vmem_limit_bytes=LIMIT
        ),
    )(lengths[:, :, 0], swap_table[:, :, 0], sequences, upstream, input_weight, output_weight)
    return pl.pallas_call(
        store_kernel,
        out_shape=tuple(jax.ShapeDtypeStruct(r.shape, r.dtype) for r in results),
        in_specs=[pl.BlockSpec(memory_space=pl.ANY)] * 4,
        out_specs=(in_hbm,) * 4,
        scratch_shapes=[pltpu.SemaphoreType.DMA((4,))],
        compiler_params=pltpu.CompilerParams(vmem_limit_bytes=8 * 1024 * 1024),
    )(*results)


def solution(mesh):
    groups, shards = mesh.shape["grp"], mesh.shape["wide"]
    split = P(("grp", "wide"), None, None)

    def whole(sequences, upstream, lengths, swap_table, input_weight, output_weight):
        sizes = groups, shards, sequences.shape[1], sequences.shape[2]
        plan = QuadPlan(*sizes) if QuadPlan.fits(*sizes) else Plan(*sizes)
        return jax.shard_map(
            functools.partial(body, plan),
            mesh=mesh,
            in_specs=(split, split, P("grp", None, None), P("grp", None, None), P(), P()),
            out_specs=(split, split, P("wide", None), P("wide", None)),
            check_vma=False,
        )(sequences, upstream, lengths, swap_table, input_weight, output_weight)

    return whole
```

```python
import functools
import math

import jax
import jax.numpy as jnp
from jax import lax
from jax.experimental import pallas as pl
from jax.experimental.pallas import tpu as pltpu
from jax.sharding import PartitionSpec as P

HEADS = 8
HEAD_DIM = 64
EPSILON = 1e-06
MODES = {'out0': 'g01,z01,G', 'out1': 'g01,z01,G'}
PARTS = {"gate": 0, "value": 1, "query": 0, "key": 1}
PART_Z = {'gate': '01', 'value': 's,01', 'query': 's,01', 'key': 's,01'}
DRAIN = ('out', 'gate', 'value', 'query', 'key', 'out0', 'out1', 'gate', 'value', 'query', 'key', 'out0', 'out1')
OUT_AT = 2
LIMIT = 67043328 - 1024 * 1024
MESH = pl.DeviceIdType.MESH
F32 = jnp.float32
BF16 = jnp.bfloat16


def dot(a, b, ca=1, cb=0):
    return lax.dot_general(a, b, (((ca,), (cb,)), ((), ())), preferred_element_type=F32)


def silu_and_slope(h):
    s = 0.5 * jnp.tanh(0.5 * h) + 0.5
    a = h * s
    return a, s + a * (1.0 - s)


def stack_heads(a, low):
    zero = jnp.zeros_like(a)
    return jnp.concatenate([jnp.where(low, a, zero), jnp.where(low, zero, a)], axis=0)


def side_by_side(a):
    half = a.shape[0] // 2
    return jnp.concatenate([a[:half], a[half:]], axis=1)


def bits_of(n):
    return n.bit_length() - 1


class Plan:
    def __init__(self, groups, shards, length, width):
        self.groups, self.shards, self.length, self.width = groups, shards, length, width
        self.chips = shards // 2
        self.share = width // shards
        self.unit = min(16, self.share)
        self.pieces = min(self.share // self.unit, groups)
        self.unit = self.share // self.pieces
        self.units = self.pieces * self.chips
        self.grp_bits = bits_of(groups)
        self.z_bits = bits_of(self.chips)
        self.q_bits = bits_of(self.pieces)
        pair = 2 * HEAD_DIM
        self.pairs = width // pair
        half = width // 2
        self.chunks = [("out%d" % i, half) for i in range(2)]
        self.chunks += [("gate%d" % i, half) for i in range(2)]
        self.chunks += [("pair%d" % p, 3 * pair) for p in range(self.pairs)]

    def stages(self, name):
        g_bits = [("g", b) for b in range(self.grp_bits)]
        z_bits = [("z", b) for b in range(self.z_bits)]
        if name not in MODES or self.q_bits != 2 or self.grp_bits != 2 or self.z_bits != 2:
            halve, rest = g_bits[: self.q_bits], g_bits[self.q_bits :]
            found = [("split", [b]) for b in halve + z_bits] + [("add", [b]) for b in rest]
            return found + ([("gather", halve)] if halve else [])
        found, halved = [], []
        for word in MODES[name].split(","):
            kind = {"g": "split", "z": "split", "a": "add", "G": "gather"}[word[0]]
            bits = [("z" if word[0] == "z" else "g", int(b)) for b in word[1:]]
            if word[0] == "g":
                halved += bits
            found.append((kind, halved if kind == "gather" else bits))
        return found

    def unit_order(self, name):
        bits = [b for kind, bits in self.stages(name) if kind == "split" for b in bits]
        whole = [("g", b) for b in range(self.q_bits) if ("g", b) not in bits]
        bits = bits + whole
        order = []
        for u in range(self.units):
            z = q = 0
            for i, (axis, b) in enumerate(bits):
                bit = (u >> (len(bits) - 1 - i)) % 2
                if axis == "z":
                    z += bit << b
                else:
                    q = q * 2 + bit
            order.append(z * self.pieces + q)
        return order

    def scratch_of(self, name, columns):
        shapes, units = [(self.units, self.unit, columns)], self.units
        for kind, bits in self.stages(name):
            if kind == "split":
                units >>= len(bits)
            if kind != "gather":
                shapes.append(((2 ** len(bits) - 1) * units, self.unit, columns))
                shapes.append((units, self.unit, columns))
            else:
                shapes.append((self.pieces, self.unit, columns))
        return shapes

    def copies(self):
        n = 5 + self.pairs
        for name, _ in self.chunks:
            for kind, bits in self.stages(name):
                n += 2 ** len(bits) - 1
        return n

    def masks(self):
        found = []
        for name, _ in self.chunks:
            for kind, bits in self.stages(name):
                for flipped in flips(bits):
                    if sorted(flipped) not in found:
                        found.append(sorted(flipped))
        top = [("z", self.z_bits - 1)]
        return found if top in found else found + [top]


def flips(bits):
    return [
        [b for i, b in enumerate(bits) if (m >> i) % 2] for m in range(1, 2 ** len(bits))
    ]


class Links:
    def __init__(self, plan, send_sem, recv_sem):
        self.send_sem, self.recv_sem, self.count, self.open = send_sem, recv_sem, 0, []
        self.g, self.w = lax.axis_index("grp"), lax.axis_index("wide")
        self.core = lax.rem(self.w, 2)
        self.z = lax.div(self.w, 2)

    def bit(self, which):
        axis, b = which
        if axis == "c":
            return self.core
        return lax.rem(lax.div(self.g if axis == "g" else self.z, 1 << b), 2)

    def partner(self, flipped):
        g, w = self.g, self.w
        for axis, b in flipped:
            step = (1 << b) * (1 - 2 * self.bit((axis, b)))
            if axis == "g":
                g = g + step
            else:
                w = w + (step if axis == "c" else 2 * step)
        return (g, w)

    def place(self, bits, flipped=()):
        at = 0
        for which in bits:
            bit = self.bit(which)
            at = at * 2 + (1 - bit if which in flipped else bit)
        return at

    def sibling(self):
        return (self.g, self.w + 1 - 2 * self.core)

    def send(self, source, target, device):
        i = self.count
        self.count += 1
        copy = pltpu.make_async_remote_copy(
            src_ref=source,
            dst_ref=target,
            send_sem=self.send_sem.at[i],
            recv_sem=self.recv_sem.at[i],
            device_id=device,
            device_id_type=MESH,
        )
        copy.start()
        self.open.append(copy)
        return copy


class Chunk:
    def __init__(self, plan, links, spec, refs, write):
        name, self.columns = spec
        self.plan, self.links, self.write = plan, links, write
        self.stages, self.order = plan.stages(name), plan.unit_order(name)
        refs = list(refs)
        self.now, self.rest = refs[0], refs[1:]
        self.units, self.step, self.copies = plan.units, 0, []

    def begin(self, lhs, rhs):
        u = self.plan.unit
        lhs = jnp.concatenate([lhs[i * u : (i + 1) * u] for i in self.order], axis=0)
        value = dot(lhs, rhs).astype(BF16)
        self.now[...] = value.reshape(self.now.shape)
        self.launch()

    def launch(self):
        kind, bits = self.stages[self.step]
        links, self.copies = self.links, []
        if kind == "gather":
            own = self.rest[0].at[pl.ds(links.place(bits), 1)]
            own[...] = self.now[...]
        for i, flipped in enumerate(flips(bits)):
            if kind == "split":
                size = self.units >> len(bits)
                source = self.now.at[pl.ds(links.place(bits, flipped) * size, size)]
                target = self.rest[0].at[pl.ds(i * size, size)]
            elif kind == "add":
                source, target = self.now, self.rest[0].at[pl.ds(i * self.units, self.units)]
            else:
                source, target = own, own
            self.copies.append(links.send(source, target, links.partner(flipped)))

    def advance(self):
        kind, bits = self.stages[self.step]
        for copy in self.copies:
            copy.wait_recv()
        if kind != "gather":
            if kind == "split":
                self.units >>= len(bits)
            size = self.units
            mine = self.links.place(bits) if kind == "split" else 0
            total = self.now[pl.ds(mine * size, size)].astype(F32)
            arrived, result = self.rest[:2]
            self.rest = self.rest[2:]
            for i in range(len(self.copies)):
                total += arrived[i * size : (i + 1) * size].astype(F32)
            result[...] = total.astype(BF16)
            self.now = result
        else:
            self.now = self.rest[0]
        self.step += 1
        if self.step < len(self.stages):
            self.launch()
            return False
        self.write(self.now[...].astype(F32).reshape(self.plan.share, self.columns))
        return True


CORE = ("c", 0)


class QuadPlan(Plan):
    def __init__(self, *sizes):
        super().__init__(*sizes)
        self.chunks = self.chunks[:2]
        self.block = self.width // 4
        self.piece = self.share // 2

    @staticmethod
    def fits(groups, shards, length, width):
        return groups == 4 and shards == 8 and width % 512 == 0 and length % 128 == 0

    def quad(self, name):
        return [("g", PARTS[name]), CORE]

    def part_stages(self, name):
        across = ("g", 1 - PARTS[name])
        named = {"s": across, "0": ("z", 0), "1": ("z", 1)}
        words = [[named[letter] for letter in word] for word in PART_Z[name].split(",")]
        last = "spread" if self.halved(name) else "share"
        return [("split", bits) for bits in words] + [(last, [across] + self.quad(name))]

    @staticmethod
    def halved(name):
        return "s" in PART_Z[name]

    def part_order(self, name):
        units = range(4 * self.chips)
        if self.halved(name):
            return units
        return [u % 2 * 2 * self.chips + u // 4 * 2 + u // 2 % 2 for u in units]

    def rows_of_units(self):
        rows = []
        for half in range(2):
            for at in range(self.chips):
                z = sum(((at >> (self.z_bits - 1 - b)) % 2) << b for b in range(self.z_bits))
                for core in range(2):
                    rows.append((2 * z + core) * self.share + half * self.piece)
        return rows

    def part_scratch(self, name):
        units = 4 * self.chips
        shapes = [(units, self.piece, self.block)]
        for kind, bits in self.part_stages(name):
            if kind == "split":
                units >>= len(bits)
                shapes.append(((2 ** len(bits) - 1) * units, self.piece, self.block))
                shapes.append((units, self.piece, self.block))
            else:
                shapes.append((8 * (1 if kind == "spread" else 2), self.piece, self.block))
        return shapes

    def copies(self):
        n = super().copies() - 5 - self.pairs + 8 + 3 * len(PARTS)
        for name in PARTS:
            n += sum(2 ** len(bits) - 1 for _, bits in self.part_stages(name))
        return n

    def masks(self):
        found = super().masks()
        for name in PARTS:
            for _, bits in self.part_stages(name):
                for flipped in flips(bits):
                    if sorted(flipped) not in found:
                        found.append(sorted(flipped))
        return [m for m in found if m != [CORE]]


class Part(Chunk):
    def __init__(self, plan, links, name, refs, write):
        self.plan, self.links, self.write, self.name = plan, links, write, name
        self.columns, self.stages = plan.block, plan.part_stages(name)
        self.now, self.rest = refs[0], list(refs[1:])
        self.units, self.step, self.copies = 4 * plan.chips, 0, []

    def begin(self, lhs, rhs):
        value = dot(lhs, rhs).astype(BF16).reshape(self.now.shape)
        for i, u in enumerate(self.plan.part_order(self.name)):
            self.now[i] = value[u]
        self.launch()

    def launch(self):
        kind, bits = self.stages[self.step]
        if kind == "split":
            return super().launch()
        links, self.copies, all_of = self.links, [], self.rest[0]
        size = 1 if kind == "spread" else 2
        own = all_of.at[pl.ds(links.place(bits) * size, size)]
        own[...] = self.now[pl.ds(links.core * size, size)]
        for flipped in flips(bits):
            core = 1 - links.core if CORE in flipped else links.core
            source = self.now.at[pl.ds(core * size, size)]
            self.copies.append(links.send(source, own, links.partner(flipped)))

    def advance(self):
        if self.stages[self.step][0] == "split":
            return super().advance()
        for copy in self.copies:
            copy.wait_recv()
        self.write(self.rest[0])
        return True


def quad_kernel(plan, scale, *refs):
    (lengths_hbm, swaps_hbm, x_hbm, up_hbm, win_hbm, wout_hbm, out_ref, dx_ref, diw_ref, dow_ref) = refs[:10]
    (win, wout, act, slope, weights, wslope, nt, gt, gt_peer, masked, masked_peer,
     blocks, held, home, arrived) = refs[10:25]
    lengths, swaps, x_ref, up_ref, load_sem, send_sem, recv_sem = refs[25:32]
    refs = list(refs[32:])
    length, width, block = plan.length, plan.width, plan.block
    pair, pairs = 2 * HEAD_DIM, plan.pairs
    links = Links(plan, send_sem, recv_sem)
    names = list(PARTS)

    barrier = pltpu.get_barrier_semaphore()
    friends = [links.sibling()]
    friends += [links.partner(flipped) for flipped in plan.masks()]
    for friend in friends:
        pl.semaphore_signal(barrier, inc=1, device_id=friend, device_id_type=MESH)
    moves = [(x_hbm, x_ref), (lengths_hbm, lengths), (up_hbm, up_ref), (swaps_hbm, swaps)]
    for j in range(4):
        columns = pl.ds(j * width, width)
        moves.append((win_hbm.at[:, columns], win.at[:, columns]))
    moves.append((wout_hbm, wout))
    loads = [pltpu.make_async_copy(a, b, load_sem.at[i]) for i, (a, b) in enumerate(moves)]
    for load in loads:
        load.start()
    for load in loads[:4]:
        load.wait()
    loads = loads[4:]

    live_count = lengths[0, links.w]
    flag = swaps[0, lax.rem(links.w, plan.shards // 2)]
    low = lax.broadcasted_iota(jnp.int32, (length, pair), 1) < HEAD_DIM
    query_at = lax.broadcasted_iota(jnp.int32, (length, length), 0)
    key_at = lax.broadcasted_iota(jnp.int32, (length, length), 1)
    allowed = (query_at >= key_at) & (key_at < live_count)
    allowed = jnp.concatenate([allowed, allowed], axis=0)

    x = x_ref[0].astype(F32)
    x_scale = lax.rsqrt(jnp.mean(x * x, axis=-1, keepdims=True) + EPSILON)
    normed = (x * x_scale).astype(BF16)
    across = (x * x_scale).astype(BF16).astype(F32).T
    piece = plan.piece
    for i, row in enumerate(plan.rows_of_units()):
        nt[0, i * piece : (i + 1) * piece] = across[row : row + piece].astype(BF16)
    row_at = lax.broadcasted_iota(jnp.int32, (length, width), 0)
    masked[...] = jnp.where(row_at < live_count, up_ref[0].astype(F32), 0.0).astype(BF16)
    pl.semaphore_wait(barrier, len(friends))
    nt_copies = {}
    for slot, flipped in ((2, [("g", 0)]), (4, [("g", 1)]), (1, [CORE])):
        nt_copies[slot] = links.send(nt.at[0], nt.at[slot], links.partner(flipped))
    masked_copy = links.send(masked, masked_peer, links.sibling())
    for j in range(4):
        loads[j].wait()
        columns = slice(j * width, (j + 1) * width)
        a, s = silu_and_slope(dot(normed, win[:, columns]))
        act[:, columns] = a.astype(BF16)
        slope[:, columns] = s

    def part(j, p):
        start = j * width + p * pair
        return act[:, start : start + pair]

    attended = []
    for p in range(pairs):
        scores = dot(stack_heads(part(2, p), low), part(3, p), 1, 1) * HEAD_DIM ** (-0.5)
        a, s = silu_and_slope(scores)
        a = jnp.where(allowed, a, 0.0).astype(BF16)
        weights[p] = a
        wslope[p] = jnp.where(allowed, s, 0.0) * HEAD_DIM ** (-0.5)
        attended.append(dot(side_by_side(a), stack_heads(part(1, p), low)))
    attended = jnp.concatenate(attended, axis=1)
    att_scale = lax.rsqrt(jnp.mean(attended * attended, axis=-1, keepdims=True) + EPSILON)
    gate = act[:, :width].astype(F32)
    att_normed = attended * att_scale
    gated = (gate * att_normed).astype(BF16)
    turned = gated.astype(F32).T
    for w in range(plan.shards):
        core, z = w % 2, w // 2
        for q in range(plan.pieces):
            row = w * plan.share + q * plan.unit
            gt[core, z * plan.pieces + q] = turned[row : row + plan.unit].astype(BF16)
    gt_copy = links.send(gt.at[1 - links.core], gt_peer, links.sibling())
    loads[4].wait()
    home[...] = (x + dot(gated, wout[...])).astype(BF16)
    home_copy = links.send(home, arrived, links.partner([("z", plan.z_bits - 1)]))

    gated_grad = dot(masked[...], wout[...], 1, 1).astype(BF16).astype(F32)
    gate_grad = (gated_grad * att_normed).astype(BF16).astype(F32)
    hg = (gate_grad * slope[:, :width]).astype(BF16)

    held_copies = {}

    def offer(name):
        j, quad = names.index(name), plan.quad(name)
        held[j, 0:1] = blocks[j, pl.ds(links.place(quad), 1)]
        copies = []
        for i, flipped in enumerate(flips(quad)):
            source = blocks.at[j, pl.ds(links.place(quad, flipped), 1)]
            target = held.at[j, pl.ds(i + 1, 1)]
            copies.append(links.send(source, target, links.partner(flipped)))
        held_copies[name] = copies

    for b in range(4):
        blocks[0, b] = hg[:, b * block : (b + 1) * block]
    offer("gate")
    norm_grad = gated_grad * gate
    along = jnp.mean(norm_grad * attended, axis=-1, keepdims=True)
    att_grad = (att_scale * norm_grad - attended * (att_scale * att_scale * att_scale * along)).astype(BF16)
    both_heads = [stack_heads(att_grad[:, p * pair : (p + 1) * pair], low) for p in range(pairs)]

    def put(j, p, grad):
        start = j * width + p * pair
        grad = (grad.astype(BF16).astype(F32) * slope[:, start : start + pair]).astype(BF16)
        blocks[j, p] = grad

    for p in range(pairs):
        put(1, p, dot(weights[p], both_heads[p], 0, 0))
    offer("value")

    chunks, flight, lines = {}, [], plan.piece

    def out_writer(i):
        half = width // 2

        def write(values):
            dow_ref[:, i * half : (i + 1) * half] = values * scale

        return write

    def part_writer(name):
        j = names.index(name)

        def write(ref):
            for m in range(8):
                row, column = (m // 4) * lines, j * width + (m % 4) * block
                if plan.halved(name):
                    total = ref[m].astype(F32)
                else:
                    i = (m % 4) * 2 + m // 4
                    total = ref[i].astype(F32) + ref[i + 8].astype(F32)
                diw_ref[row : row + lines, column : column + block] = total * scale

        return write

    for i, spec in enumerate(plan.chunks):
        n = len(plan.scratch_of(*spec))
        chunks[spec[0]] = Chunk(plan, links, spec, refs[:n], out_writer(i))
        refs = refs[n:]
    for name in names:
        n = len(plan.part_scratch(name))
        chunks[name] = Part(plan, links, name, refs[:n], part_writer(name))
        refs = refs[n:]

    def begin_out():
        masked_copy.wait_recv()
        gt_copy.wait_recv()
        mine = gt[pl.ds(links.core, 1)].reshape(width // 2, length)
        lhs = jnp.concatenate([mine, gt_peer[...].reshape(width // 2, length)], axis=1)
        for i in range(2):
            columns = slice(i * (width // 2), (i + 1) * (width // 2))
            chunks["out%d" % i].begin(lhs, jnp.concatenate([masked[:, columns], masked_peer[:, columns]], axis=0))
            flight.append("out%d" % i)

    if OUT_AT == 0:
        begin_out()
    score_grads = []
    for p in range(pairs):
        weight_grad = dot(both_heads[p], part(1, p), 1, 1).astype(BF16).astype(F32)
        score_grads.append((weight_grad * wslope[p]).astype(BF16))
        put(2, p, dot(side_by_side(score_grads[p]), stack_heads(part(3, p), low)))
    offer("query")
    for p in range(pairs):
        put(3, p, dot(score_grads[p], stack_heads(part(2, p), low), 0, 0))
    offer("key")

    if OUT_AT == 1:
        begin_out()
    for slot in (2, 4):
        nt_copies[slot].wait_recv()
        nt_copies[slot + 1] = links.send(nt.at[slot], nt.at[slot + 1], links.sibling())

    back = 0.0
    for j in range(4):
        grads = jnp.concatenate([blocks[j, b] for b in range(4)], axis=1)
        back += dot(grads, win[:, j * width : (j + 1) * width], 1, 1)
    along = jnp.mean(back * x, axis=-1, keepdims=True)
    dx = x_scale * back - x * (x_scale * x_scale * x_scale * along)
    dx_ref[0] = (masked[...].astype(F32) + dx).astype(BF16)

    waited = []

    def begin(name):
        slots = [0, 1, 2, 3] if PARTS[name] == 0 else [0, 1, 4, 5]
        for slot in slots[1:]:
            if slot % 2 and slot not in waited:
                waited.append(slot)
                nt_copies[slot].wait_recv()
        for copy in held_copies[name]:
            copy.wait_recv()
        order = [slots[0], slots[2], slots[1], slots[3]]
        lhs = jnp.concatenate([nt[slot] for slot in order], axis=1)
        chunks[name].begin(lhs, held[names.index(name)].reshape(4 * length, block))

    started = []

    def step(name):
        if name == "out":
            return begin_out()
        if name in PARTS and name not in started:
            started.append(name)
            begin(name)
            flight.append(name)
            return
        flight.remove(name)
        if not chunks[name].advance():
            flight.append(name)

    for name in DRAIN:
        step(name)
    for name in names:
        if name not in started:
            step(name)
    while flight:
        step(flight[0])
    home_copy.wait_recv()
    out_ref[0] = jnp.where(flag == 1, arrived[...].astype(F32), home[...].astype(F32)).astype(BF16)
    for copy in links.open:
        copy.wait_send()


def kernel(plan, scale, *refs):
    (lengths_hbm, swaps_hbm, x_hbm, up_hbm, win_hbm, wout_hbm, out_ref, dx_ref, diw_ref, dow_ref) = refs[:10]
    (win, wout, act, slope, weights, wslope, nt, nt_peer, gt, gt_peer, masked, masked_peer,
     hg_gate, hg_gate_peer, hg_pair, hg_pair_peer, home, arrived) = refs[10:28]
    lengths, swaps, x_ref, up_ref, load_sem, send_sem, recv_sem = refs[28:35]
    refs = list(refs[35:])
    length, width = plan.length, plan.width
    pair, pairs = 2 * HEAD_DIM, plan.pairs
    links = Links(plan, send_sem, recv_sem)

    barrier = pltpu.get_barrier_semaphore()
    friends = [links.sibling()]
    friends += [links.partner(flipped) for flipped in plan.masks()]
    for friend in friends:
        pl.semaphore_signal(barrier, inc=1, device_id=friend, device_id_type=MESH)
    moves = [(x_hbm, x_ref), (lengths_hbm, lengths), (up_hbm, up_ref), (swaps_hbm, swaps)]
    for j in range(4):
        columns = pl.ds(j * width, width)
        moves.append((win_hbm.at[:, columns], win.at[:, columns]))
    moves.append((wout_hbm, wout))
    loads = [pltpu.make_async_copy(a, b, load_sem.at[i]) for i, (a, b) in enumerate(moves)]
    for load in loads:
        load.start()
    for load in loads[:4]:
        load.wait()
    loads = loads[4:]

    live_count = lengths[0, links.w]
    flag = swaps[0, lax.rem(links.w, plan.shards // 2)]
    low = lax.broadcasted_iota(jnp.int32, (length, pair), 1) < HEAD_DIM
    query_at = lax.broadcasted_iota(jnp.int32, (length, length), 0)
    key_at = lax.broadcasted_iota(jnp.int32, (length, length), 1)
    allowed = (query_at >= key_at) & (key_at < live_count)
    allowed = jnp.concatenate([allowed, allowed], axis=0)

    def split_rows(values, target):
        across = values.astype(F32).T
        for w in range(plan.shards):
            core, z = w % 2, w // 2
            for q in range(plan.pieces):
                row = w * plan.share + q * plan.unit
                target[core, z * plan.pieces + q] = across[row : row + plan.unit].astype(BF16)

    def both(own, peer):
        mine = own[pl.ds(links.core, 1)].reshape(width // 2, length)
        return jnp.concatenate([mine, peer[...].reshape(width // 2, length)], axis=1)

    x = x_ref[0].astype(F32)
    x_scale = lax.rsqrt(jnp.mean(x * x, axis=-1, keepdims=True) + EPSILON)
    normed = (x * x_scale).astype(BF16)
    row_at = lax.broadcasted_iota(jnp.int32, (length, width), 0)
    masked[...] = jnp.where(row_at < live_count, up_ref[0].astype(F32), 0.0).astype(BF16)
    split_rows(normed, nt)
    pl.semaphore_wait(barrier, len(friends))
    masked_copy = links.send(masked, masked_peer, links.sibling())
    nt_copy = links.send(nt.at[1 - links.core], nt_peer, links.sibling())
    for j in range(4):
        loads[j].wait()
        columns = slice(j * width, (j + 1) * width)
        a, s = silu_and_slope(dot(normed, win[:, columns]))
        act[:, columns] = a.astype(BF16)
        slope[:, columns] = s

    def part(j, p):
        start = j * width + p * pair
        return act[:, start : start + pair]

    attended = []
    for p in range(pairs):
        scores = dot(stack_heads(part(2, p), low), part(3, p), 1, 1) * HEAD_DIM ** (-0.5)
        a, s = silu_and_slope(scores)
        a = jnp.where(allowed, a, 0.0).astype(BF16)
        weights[p] = a
        wslope[p] = jnp.where(allowed, s, 0.0) * HEAD_DIM ** (-0.5)
        attended.append(dot(side_by_side(a), stack_heads(part(1, p), low)))
    attended = jnp.concatenate(attended, axis=1)
    att_scale = lax.rsqrt(jnp.mean(attended * attended, axis=-1, keepdims=True) + EPSILON)
    gate = act[:, :width].astype(F32)
    att_normed = attended * att_scale
    gated = (gate * att_normed).astype(BF16)
    split_rows(gated, gt)
    gt_copy = links.send(gt.at[1 - links.core], gt_peer, links.sibling())
    loads[4].wait()
    home[...] = (x + dot(gated, wout[...])).astype(BF16)
    home_copy = links.send(home, arrived, links.partner([("z", plan.z_bits - 1)]))

    gated_grad = dot(masked[...], wout[...], 1, 1).astype(BF16).astype(F32)
    gate_grad = (gated_grad * att_normed).astype(BF16).astype(F32)
    hg_gate[...] = (gate_grad * slope[:, :width]).astype(BF16)
    hg_gate_copy = links.send(hg_gate, hg_gate_peer, links.sibling())
    norm_grad = gated_grad * gate
    along = jnp.mean(norm_grad * attended, axis=-1, keepdims=True)
    att_grad = (att_scale * norm_grad - attended * (att_scale * att_scale * att_scale * along)).astype(BF16)

    chunks, flight = {}, []

    def writer(name):
        kind, i = name.rstrip("0123456789"), int(name[-1])
        half = width // 2

        def write(values):
            values = values * scale
            if kind == "out":
                dow_ref[:, i * half : (i + 1) * half] = values
            elif kind == "gate":
                diw_ref[:, i * half : (i + 1) * half] = values
            else:
                for j in range(3):
                    start = (j + 1) * width + i * pair
                    diw_ref[:, start : start + pair] = values[:, j * pair : (j + 1) * pair]

        return write

    for spec in plan.chunks:
        n = len(plan.scratch_of(*spec))
        chunks[spec[0]] = Chunk(plan, links, spec, refs[:n], writer(spec[0]))
        refs = refs[n:]

    def begin(name, lhs, rhs):
        chunks[name].begin(lhs, rhs)
        flight.append(chunks[name])

    def advance(count):
        for _ in range(min(count, len(flight))):
            chunk = flight.pop(0)
            if not chunk.advance():
                flight.append(chunk)

    masked_copy.wait_recv()
    gt_copy.wait_recv()
    lhs = both(gt, gt_peer)
    for i in range(2):
        columns = slice(i * (width // 2), (i + 1) * (width // 2))
        begin("out%d" % i, lhs, jnp.concatenate([masked[:, columns], masked_peer[:, columns]], axis=0))

    pair_copies = []

    def pair_backward(p):
        q, k, v = part(2, p), part(3, p), part(1, p)
        q2 = stack_heads(q, low)
        da2 = stack_heads(att_grad[:, p * pair : (p + 1) * pair], low)
        weight_grad = dot(da2, v, 1, 1).astype(BF16).astype(F32)
        score_grad = (weight_grad * wslope[p]).astype(BF16)
        dv = dot(weights[p], da2, 0, 0)
        dq = dot(side_by_side(score_grad), stack_heads(k, low))
        dk = dot(score_grad, q2, 0, 0)
        for j, grad in enumerate((dv, dq, dk)):
            start = (j + 1) * width + p * pair
            grad = grad.astype(BF16).astype(F32) * slope[:, start : start + pair]
            hg_pair[p, :, j * pair : (j + 1) * pair] = grad.astype(BF16)
        pair_copies.append(links.send(hg_pair.at[p], hg_pair_peer.at[p], links.sibling()))

    def begin_pair(p):
        pair_copies[p].wait_recv()
        begin("pair%d" % p, lhs_in, jnp.concatenate([hg_pair[p], hg_pair_peer[p]], axis=0))

    pair_backward(0)
    hg_gate_copy.wait_recv()
    nt_copy.wait_recv()
    lhs_in = both(nt, nt_peer)
    for i in range(2):
        columns = slice(i * (width // 2), (i + 1) * (width // 2))
        begin("gate%d" % i, lhs_in, jnp.concatenate([hg_gate[:, columns], hg_gate_peer[:, columns]], axis=0))
    for p in range(1, pairs):
        pair_backward(p)
        begin_pair(p - 1)

    back = dot(hg_gate[...], win[:, :width], 1, 1)
    for p in range(pairs):
        if p == 1:
            begin_pair(pairs - 1)
        for j in range(3):
            start = (j + 1) * width + p * pair
            back += dot(hg_pair[p, :, j * pair : (j + 1) * pair], win[:, start : start + pair], 1, 1)
    along = jnp.mean(back * x, axis=-1, keepdims=True)
    dx = x_scale * back - x * (x_scale * x_scale * x_scale * along)
    dx_ref[0] = (masked[...].astype(F32) + dx).astype(BF16)

    while flight:
        advance(1)
    home_copy.wait_recv()
    out_ref[0] = jnp.where(flag == 1, arrived[...].astype(F32), home[...].astype(F32)).astype(BF16)
    for copy in links.open:
        copy.wait_send()


def store_kernel(*refs):
    sems = refs[8]
    copies = [pltpu.make_async_copy(refs[i], refs[4 + i], sems.at[i]) for i in range(4)]
    for copy in copies:
        copy.start()
    for copy in copies:
        copy.wait()


def body(plan, sequences, upstream, lengths, swap_table, input_weight, output_weight):
    length, width = plan.length, plan.width
    scale = 1.0 / math.sqrt(length * plan.shards * plan.groups)
    rows = plan.units, plan.unit, length
    pair, pairs = 2 * HEAD_DIM, plan.pairs
    vmem = lambda *shape: pltpu.VMEM(shape, BF16)
    quad = isinstance(plan, QuadPlan)
    if quad:
        exchanged = [
            vmem(6, width, length),
            vmem(2, *rows),
            vmem(*rows),
            vmem(length, width),
            vmem(length, width),
            vmem(4, 4, length, plan.block),
            vmem(4, 4, length, plan.block),
        ]
    else:
        exchanged = [
            vmem(2, *rows),
            vmem(*rows),
            vmem(2, *rows),
            vmem(*rows),
            vmem(length, width),
            vmem(length, width),
            vmem(length, width),
            vmem(length, width),
            vmem(pairs, length, 3 * pair),
            vmem(pairs, length, 3 * pair),
        ]
    scratch = [
        vmem(width, 4 * width),
        vmem(width, width),
        vmem(length, 4 * width),
        pltpu.VMEM((length, 4 * width), F32),
        vmem(pairs, 2 * length, length),
        pltpu.VMEM((pairs, 2 * length, length), F32),
        *exchanged,
        vmem(length, width),
        vmem(length, width),
        pltpu.SMEM((1, plan.shards), jnp.int32),
        pltpu.SMEM((1, plan.shards // 2), jnp.int32),
        vmem(1, length, width),
        vmem(1, length, width),
        pltpu.SemaphoreType.DMA((9,)),
        pltpu.SemaphoreType.DMA((plan.copies(),)),
        pltpu.SemaphoreType.DMA((plan.copies(),)),
    ]
    for spec in plan.chunks:
        scratch += [vmem(*shape) for shape in plan.scratch_of(*spec)]
    for name in PARTS if quad else ():
        scratch += [vmem(*shape) for shape in plan.part_scratch(name)]
    in_vmem = pl.BlockSpec(memory_space=pltpu.VMEM)
    in_hbm = pl.BlockSpec(memory_space=pltpu.HBM)
    results = pl.pallas_call(
        functools.partial(quad_kernel if quad else kernel, plan, scale),
        out_shape=(
            pltpu.VMEM(sequences.shape, BF16),
            pltpu.VMEM(sequences.shape, BF16),
            pltpu.VMEM((plan.share, 4 * width), F32),
            pltpu.VMEM((plan.share, width), F32),
        ),
        in_specs=[in_hbm] * 6,
        out_specs=(in_vmem,) * 4,
        scratch_shapes=scratch,
        compiler_params=pltpu.CompilerParams(
            collective_id=0, has_side_effects=True, vmem_limit_bytes=LIMIT
        ),
    )(lengths[:, :, 0], swap_table[:, :, 0], sequences, upstream, input_weight, output_weight)
    return pl.pallas_call(
        store_kernel,
        out_shape=tuple(jax.ShapeDtypeStruct(r.shape, r.dtype) for r in results),
        in_specs=[pl.BlockSpec(memory_space=pl.ANY)] * 4,
        out_specs=(in_hbm,) * 4,
        scratch_shapes=[pltpu.SemaphoreType.DMA((4,))],
        compiler_params=pltpu.CompilerParams(vmem_limit_bytes=8 * 1024 * 1024),
    )(*results)


def solution(mesh):
    groups, shards = mesh.shape["grp"], mesh.shape["wide"]
    split = P(("grp", "wide"), None, None)

    def whole(sequences, upstream, lengths, swap_table, input_weight, output_weight):
        sizes = groups, shards, sequences.shape[1], sequences.shape[2]
        plan = QuadPlan(*sizes) if QuadPlan.fits(*sizes) else Plan(*sizes)
        return jax.shard_map(
            functools.partial(body, plan),
            mesh=mesh,
            in_specs=(split, split, P("grp", None, None), P("grp", None, None), P(), P()),
            out_specs=(split, split, P("wide", None), P("wide", None)),
            check_vma=False,
        )(sequences, upstream, lengths, swap_table, input_weight, output_weight)

    return whole
```

```python
import functools
import math

import jax
import jax.numpy as jnp
from jax import lax
from jax.experimental import pallas as pl
from jax.experimental.pallas import tpu as pltpu
from jax.sharding import PartitionSpec as P

HEADS = 8
HEAD_DIM = 64
EPSILON = 1e-06
MODES = {'out0': 'g01,z01,G', 'out1': 'g01,z01,G'}
PARTS = {"gate": 0, "value": 1, "query": 0, "key": 1}
PART_Z = {'gate': '01', 'value': 's,01', 'query': 's,01', 'key': 's,01'}
DRAIN = ('out', 'gate', 'value', 'query', 'key', 'out0', 'out1', 'value', 'gate', 'query', 'key', 'out0', 'out1', 'value', 'query', 'key')
OUT_AT = 2
LIMIT = 67043328 - 1024 * 1024
MESH = pl.DeviceIdType.MESH
F32 = jnp.float32
BF16 = jnp.bfloat16


def dot(a, b, ca=1, cb=0):
    return lax.dot_general(a, b, (((ca,), (cb,)), ((), ())), preferred_element_type=F32)


def silu_and_slope(h):
    s = 0.5 * jnp.tanh(0.5 * h) + 0.5
    a = h * s
    return a, s + a * (1.0 - s)


def stack_heads(a, low):
    zero = jnp.zeros_like(a)
    return jnp.concatenate([jnp.where(low, a, zero), jnp.where(low, zero, a)], axis=0)


def side_by_side(a):
    half = a.shape[0] // 2
    return jnp.concatenate([a[:half], a[half:]], axis=1)


def bits_of(n):
    return n.bit_length() - 1


class Plan:
    def __init__(self, groups, shards, length, width):
        self.groups, self.shards, self.length, self.width = groups, shards, length, width
        self.chips = shards // 2
        self.share = width // shards
        self.unit = min(16, self.share)
        self.pieces = min(self.share // self.unit, groups)
        self.unit = self.share // self.pieces
        self.units = self.pieces * self.chips
        self.grp_bits = bits_of(groups)
        self.z_bits = bits_of(self.chips)
        self.q_bits = bits_of(self.pieces)
        pair = 2 * HEAD_DIM
        self.pairs = width // pair
        half = width // 2
        self.chunks = [("out%d" % i, half) for i in range(2)]
        self.chunks += [("gate%d" % i, half) for i in range(2)]
        self.chunks += [("pair%d" % p, 3 * pair) for p in range(self.pairs)]

    def stages(self, name):
        g_bits = [("g", b) for b in range(self.grp_bits)]
        z_bits = [("z", b) for b in range(self.z_bits)]
        if name not in MODES or self.q_bits != 2 or self.grp_bits != 2 or self.z_bits != 2:
            halve, rest = g_bits[: self.q_bits], g_bits[self.q_bits :]
            found = [("split", [b]) for b in halve + z_bits] + [("add", [b]) for b in rest]
            return found + ([("gather", halve)] if halve else [])
        found, halved = [], []
        for word in MODES[name].split(","):
            kind = {"g": "split", "z": "split", "a": "add", "G": "gather"}[word[0]]
            bits = [("z" if word[0] == "z" else "g", int(b)) for b in word[1:]]
            if word[0] == "g":
                halved += bits
            found.append((kind, halved if kind == "gather" else bits))
        return found

    def unit_order(self, name):
        bits = [b for kind, bits in self.stages(name) if kind == "split" for b in bits]
        whole = [("g", b) for b in range(self.q_bits) if ("g", b) not in bits]
        bits = bits + whole
        order = []
        for u in range(self.units):
            z = q = 0
            for i, (axis, b) in enumerate(bits):
                bit = (u >> (len(bits) - 1 - i)) % 2
                if axis == "z":
                    z += bit << b
                else:
                    q = q * 2 + bit
            order.append(z * self.pieces + q)
        return order

    def scratch_of(self, name, columns):
        shapes, units = [(self.units, self.unit, columns)], self.units
        for kind, bits in self.stages(name):
            if kind == "split":
                units >>= len(bits)
            if kind != "gather":
                shapes.append(((2 ** len(bits) - 1) * units, self.unit, columns))
                shapes.append((units, self.unit, columns))
            else:
                shapes.append((self.pieces, self.unit, columns))
        return shapes

    def copies(self):
        n = 5 + self.pairs
        for name, _ in self.chunks:
            for kind, bits in self.stages(name):
                n += 2 ** len(bits) - 1
        return n

    def masks(self):
        found = []
        for name, _ in self.chunks:
            for kind, bits in self.stages(name):
                for flipped in flips(bits):
                    if sorted(flipped) not in found:
                        found.append(sorted(flipped))
        top = [("z", self.z_bits - 1)]
        return found if top in found else found + [top]


def flips(bits):
    return [
        [b for i, b in enumerate(bits) if (m >> i) % 2] for m in range(1, 2 ** len(bits))
    ]


class Links:
    def __init__(self, plan, send_sem, recv_sem):
        self.send_sem, self.recv_sem, self.count, self.open = send_sem, recv_sem, 0, []
        self.g, self.w = lax.axis_index("grp"), lax.axis_index("wide")
        self.core = lax.rem(self.w, 2)
        self.z = lax.div(self.w, 2)

    def bit(self, which):
        axis, b = which
        if axis == "c":
            return self.core
        return lax.rem(lax.div(self.g if axis == "g" else self.z, 1 << b), 2)

    def partner(self, flipped):
        g, w = self.g, self.w
        for axis, b in flipped:
            step = (1 << b) * (1 - 2 * self.bit((axis, b)))
            if axis == "g":
                g = g + step
            else:
                w = w + (step if axis == "c" else 2 * step)
        return (g, w)

    def place(self, bits, flipped=()):
        at = 0
        for which in bits:
            bit = self.bit(which)
            at = at * 2 + (1 - bit if which in flipped else bit)
        return at

    def sibling(self):
        return (self.g, self.w + 1 - 2 * self.core)

    def send(self, source, target, device):
        i = self.count
        self.count += 1
        copy = pltpu.make_async_remote_copy(
            src_ref=source,
            dst_ref=target,
            send_sem=self.send_sem.at[i],
            recv_sem=self.recv_sem.at[i],
            device_id=device,
            device_id_type=MESH,
        )
        copy.start()
        self.open.append(copy)
        return copy


class Chunk:
    def __init__(self, plan, links, spec, refs, write):
        name, self.columns = spec
        self.plan, self.links, self.write = plan, links, write
        self.stages, self.order = plan.stages(name), plan.unit_order(name)
        refs = list(refs)
        self.now, self.rest = refs[0], refs[1:]
        self.units, self.step, self.copies = plan.units, 0, []

    def begin(self, lhs, rhs):
        u = self.plan.unit
        lhs = jnp.concatenate([lhs[i * u : (i + 1) * u] for i in self.order], axis=0)
        value = dot(lhs, rhs).astype(BF16)
        self.now[...] = value.reshape(self.now.shape)
        self.launch()

    def launch(self):
        kind, bits = self.stages[self.step]
        links, self.copies = self.links, []
        if kind == "gather":
            own = self.rest[0].at[pl.ds(links.place(bits), 1)]
            own[...] = self.now[...]
        for i, flipped in enumerate(flips(bits)):
            if kind == "split":
                size = self.units >> len(bits)
                source = self.now.at[pl.ds(links.place(bits, flipped) * size, size)]
                target = self.rest[0].at[pl.ds(i * size, size)]
            elif kind == "add":
                source, target = self.now, self.rest[0].at[pl.ds(i * self.units, self.units)]
            else:
                source, target = own, own
            self.copies.append(links.send(source, target, links.partner(flipped)))

    def advance(self):
        kind, bits = self.stages[self.step]
        for copy in self.copies:
            copy.wait_recv()
        if kind != "gather":
            if kind == "split":
                self.units >>= len(bits)
            size = self.units
            mine = self.links.place(bits) if kind == "split" else 0
            total = self.now[pl.ds(mine * size, size)].astype(F32)
            arrived, result = self.rest[:2]
            self.rest = self.rest[2:]
            for i in range(len(self.copies)):
                total += arrived[i * size : (i + 1) * size].astype(F32)
            result[...] = total.astype(BF16)
            self.now = result
        else:
            self.now = self.rest[0]
        self.step += 1
        if self.step < len(self.stages):
            self.launch()
            return False
        self.write(self.now[...].astype(F32).reshape(self.plan.share, self.columns))
        return True


CORE = ("c", 0)


class QuadPlan(Plan):
    def __init__(self, *sizes):
        super().__init__(*sizes)
        self.chunks = self.chunks[:2]
        self.block = self.width // 4
        self.piece = self.share // 2

    @staticmethod
    def fits(groups, shards, length, width):
        return groups == 4 and shards == 8 and width % 512 == 0 and length % 128 == 0

    def quad(self, name):
        return [("g", PARTS[name]), CORE]

    def part_stages(self, name):
        across = ("g", 1 - PARTS[name])
        named = {"s": across, "0": ("z", 0), "1": ("z", 1)}
        words = [[named[letter] for letter in word] for word in PART_Z[name].split(",")]
        last = "spread" if self.halved(name) else "share"
        return [("split", bits) for bits in words] + [(last, [across] + self.quad(name))]

    @staticmethod
    def halved(name):
        return "s" in PART_Z[name]

    def part_order(self, name):
        units = range(4 * self.chips)
        if self.halved(name):
            return units
        return [u % 2 * 2 * self.chips + u // 4 * 2 + u // 2 % 2 for u in units]

    def rows_of_units(self):
        rows = []
        for half in range(2):
            for at in range(self.chips):
                z = sum(((at >> (self.z_bits - 1 - b)) % 2) << b for b in range(self.z_bits))
                for core in range(2):
                    rows.append((2 * z + core) * self.share + half * self.piece)
        return rows

    def part_scratch(self, name):
        units = 4 * self.chips
        shapes = [(units, self.piece, self.block)]
        for kind, bits in self.part_stages(name):
            if kind == "split":
                units >>= len(bits)
                shapes.append(((2 ** len(bits) - 1) * units, self.piece, self.block))
                shapes.append((units, self.piece, self.block))
            else:
                shapes.append((8 * (1 if kind == "spread" else 2), self.piece, self.block))
        return shapes

    def copies(self):
        n = super().copies() - 5 - self.pairs + 8 + 3 * len(PARTS)
        for name in PARTS:
            n += sum(2 ** len(bits) - 1 for _, bits in self.part_stages(name))
        return n

    def masks(self):
        found = super().masks()
        for name in PARTS:
            for _, bits in self.part_stages(name):
                for flipped in flips(bits):
                    if sorted(flipped) not in found:
                        found.append(sorted(flipped))
        return [m for m in found if m != [CORE]]


class Part(Chunk):
    def __init__(self, plan, links, name, refs, write):
        self.plan, self.links, self.write, self.name = plan, links, write, name
        self.columns, self.stages = plan.block, plan.part_stages(name)
        self.now, self.rest = refs[0], list(refs[1:])
        self.units, self.step, self.copies = 4 * plan.chips, 0, []

    def begin(self, lhs, rhs):
        value = dot(lhs, rhs).astype(BF16).reshape(self.now.shape)
        for i, u in enumerate(self.plan.part_order(self.name)):
            self.now[i] = value[u]
        self.launch()

    def launch(self):
        kind, bits = self.stages[self.step]
        if kind == "split":
            return super().launch()
        links, self.copies, all_of = self.links, [], self.rest[0]
        size = 1 if kind == "spread" else 2
        own = all_of.at[pl.ds(links.place(bits) * size, size)]
        own[...] = self.now[pl.ds(links.core * size, size)]
        for flipped in flips(bits):
            core = 1 - links.core if CORE in flipped else links.core
            source = self.now.at[pl.ds(core * size, size)]
            self.copies.append(links.send(source, own, links.partner(flipped)))

    def advance(self):
        if self.stages[self.step][0] == "split":
            return super().advance()
        for copy in self.copies:
            copy.wait_recv()
        self.write(self.rest[0])
        return True


def quad_kernel(plan, scale, *refs):
    (lengths_hbm, swaps_hbm, x_hbm, up_hbm, win_hbm, wout_hbm, out_ref, dx_ref, diw_ref, dow_ref) = refs[:10]
    (win, wout, act, slope, weights, wslope, nt, gt, gt_peer, masked, masked_peer,
     blocks, held, home, arrived) = refs[10:25]
    lengths, swaps, x_ref, up_ref, load_sem, send_sem, recv_sem = refs[25:32]
    refs = list(refs[32:])
    length, width, block = plan.length, plan.width, plan.block
    pair, pairs = 2 * HEAD_DIM, plan.pairs
    links = Links(plan, send_sem, recv_sem)
    names = list(PARTS)

    barrier = pltpu.get_barrier_semaphore()
    friends = [links.sibling()]
    friends += [links.partner(flipped) for flipped in plan.masks()]
    for friend in friends:
        pl.semaphore_signal(barrier, inc=1, device_id=friend, device_id_type=MESH)
    moves = [(x_hbm, x_ref), (lengths_hbm, lengths), (up_hbm, up_ref), (swaps_hbm, swaps)]
    for j in range(4):
        columns = pl.ds(j * width, width)
        moves.append((win_hbm.at[:, columns], win.at[:, columns]))
    moves.append((wout_hbm, wout))
    loads = [pltpu.make_async_copy(a, b, load_sem.at[i]) for i, (a, b) in enumerate(moves)]
    for load in loads:
        load.start()
    for load in loads[:4]:
        load.wait()
    loads = loads[4:]

    live_count = lengths[0, links.w]
    flag = swaps[0, lax.rem(links.w, plan.shards // 2)]
    low = lax.broadcasted_iota(jnp.int32, (length, pair), 1) < HEAD_DIM
    query_at = lax.broadcasted_iota(jnp.int32, (length, length), 0)
    key_at = lax.broadcasted_iota(jnp.int32, (length, length), 1)
    allowed = (query_at >= key_at) & (key_at < live_count)
    allowed = jnp.concatenate([allowed, allowed], axis=0)

    x = x_ref[0].astype(F32)
    x_scale = lax.rsqrt(jnp.mean(x * x, axis=-1, keepdims=True) + EPSILON)
    normed = (x * x_scale).astype(BF16)
    across = (x * x_scale).astype(BF16).astype(F32).T
    piece = plan.piece
    for i, row in enumerate(plan.rows_of_units()):
        nt[0, i * piece : (i + 1) * piece] = across[row : row + piece].astype(BF16)
    row_at = lax.broadcasted_iota(jnp.int32, (length, width), 0)
    masked[...] = jnp.where(row_at < live_count, up_ref[0].astype(F32), 0.0).astype(BF16)
    pl.semaphore_wait(barrier, len(friends))
    nt_copies = {}
    for slot, flipped in ((2, [("g", 0)]), (4, [("g", 1)]), (1, [CORE])):
        nt_copies[slot] = links.send(nt.at[0], nt.at[slot], links.partner(flipped))
    masked_copy = links.send(masked, masked_peer, links.sibling())
    for j in range(4):
        loads[j].wait()
        columns = slice(j * width, (j + 1) * width)
        a, s = silu_and_slope(dot(normed, win[:, columns]))
        act[:, columns] = a.astype(BF16)
        slope[:, columns] = s

    def part(j, p):
        start = j * width + p * pair
        return act[:, start : start + pair]

    attended = []
    for p in range(pairs):
        scores = dot(stack_heads(part(2, p), low), part(3, p), 1, 1) * HEAD_DIM ** (-0.5)
        a, s = silu_and_slope(scores)
        a = jnp.where(allowed, a, 0.0).astype(BF16)
        weights[p] = a
        wslope[p] = jnp.where(allowed, s, 0.0) * HEAD_DIM ** (-0.5)
        attended.append(dot(side_by_side(a), stack_heads(part(1, p), low)))
    attended = jnp.concatenate(attended, axis=1)
    att_scale = lax.rsqrt(jnp.mean(attended * attended, axis=-1, keepdims=True) + EPSILON)
    gate = act[:, :width].astype(F32)
    att_normed = attended * att_scale
    gated = (gate * att_normed).astype(BF16)
    turned = gated.astype(F32).T
    for w in range(plan.shards):
        core, z = w % 2, w // 2
        for q in range(plan.pieces):
            row = w * plan.share + q * plan.unit
            gt[core, z * plan.pieces + q] = turned[row : row + plan.unit].astype(BF16)
    gt_copy = links.send(gt.at[1 - links.core], gt_peer, links.sibling())
    loads[4].wait()
    home[...] = (x + dot(gated, wout[...])).astype(BF16)
    home_copy = links.send(home, arrived, links.partner([("z", plan.z_bits - 1)]))

    gated_grad = dot(masked[...], wout[...], 1, 1).astype(BF16).astype(F32)
    gate_grad = (gated_grad * att_normed).astype(BF16).astype(F32)
    hg = (gate_grad * slope[:, :width]).astype(BF16)

    held_copies = {}

    def offer(name):
        j, quad = names.index(name), plan.quad(name)
        held[j, 0:1] = blocks[j, pl.ds(links.place(quad), 1)]
        copies = []
        for i, flipped in enumerate(flips(quad)):
            source = blocks.at[j, pl.ds(links.place(quad, flipped), 1)]
            target = held.at[j, pl.ds(i + 1, 1)]
            copies.append(links.send(source, target, links.partner(flipped)))
        held_copies[name] = copies

    for b in range(4):
        blocks[0, b] = hg[:, b * block : (b + 1) * block]
    offer("gate")
    norm_grad = gated_grad * gate
    along = jnp.mean(norm_grad * attended, axis=-1, keepdims=True)
    att_grad = (att_scale * norm_grad - attended * (att_scale * att_scale * att_scale * along)).astype(BF16)
    both_heads = [stack_heads(att_grad[:, p * pair : (p + 1) * pair], low) for p in range(pairs)]

    def put(j, p, grad):
        start = j * width + p * pair
        grad = (grad.astype(BF16).astype(F32) * slope[:, start : start + pair]).astype(BF16)
        blocks[j, p] = grad

    for p in range(pairs):
        put(1, p, dot(weights[p], both_heads[p], 0, 0))
    offer("value")

    chunks, flight, lines = {}, [], plan.piece

    def out_writer(i):
        half = width // 2

        def write(values):
            dow_ref[:, i * half : (i + 1) * half] = values * scale

        return write

    def part_writer(name):
        j = names.index(name)

        def write(ref):
            for m in range(8):
                row, column = (m // 4) * lines, j * width + (m % 4) * block
                if plan.halved(name):
                    total = ref[m].astype(F32)
                else:
                    i = (m % 4) * 2 + m // 4
                    total = ref[i].astype(F32) + ref[i + 8].astype(F32)
                diw_ref[row : row + lines, column : column + block] = total * scale

        return write

    for i, spec in enumerate(plan.chunks):
        n = len(plan.scratch_of(*spec))
        chunks[spec[0]] = Chunk(plan, links, spec, refs[:n], out_writer(i))
        refs = refs[n:]
    for name in names:
        n = len(plan.part_scratch(name))
        chunks[name] = Part(plan, links, name, refs[:n], part_writer(name))
        refs = refs[n:]

    def begin_out():
        masked_copy.wait_recv()
        gt_copy.wait_recv()
        mine = gt[pl.ds(links.core, 1)].reshape(width // 2, length)
        lhs = jnp.concatenate([mine, gt_peer[...].reshape(width // 2, length)], axis=1)
        for i in range(2):
            columns = slice(i * (width // 2), (i + 1) * (width // 2))
            chunks["out%d" % i].begin(lhs, jnp.concatenate([masked[:, columns], masked_peer[:, columns]], axis=0))
            flight.append("out%d" % i)

    if OUT_AT == 0:
        begin_out()
    score_grads = []
    for p in range(pairs):
        weight_grad = dot(both_heads[p], part(1, p), 1, 1).astype(BF16).astype(F32)
        score_grads.append((weight_grad * wslope[p]).astype(BF16))
        put(2, p, dot(side_by_side(score_grads[p]), stack_heads(part(3, p), low)))
    offer("query")
    for p in range(pairs):
        put(3, p, dot(score_grads[p], stack_heads(part(2, p), low), 0, 0))
    offer("key")

    if OUT_AT == 1:
        begin_out()
    for slot in (2, 4):
        nt_copies[slot].wait_recv()
        nt_copies[slot + 1] = links.send(nt.at[slot], nt.at[slot + 1], links.sibling())

    back = 0.0
    for j in range(4):
        grads = jnp.concatenate([blocks[j, b] for b in range(4)], axis=1)
        back += dot(grads, win[:, j * width : (j + 1) * width], 1, 1)
    along = jnp.mean(back * x, axis=-1, keepdims=True)
    dx = x_scale * back - x * (x_scale * x_scale * x_scale * along)
    dx_ref[0] = (masked[...].astype(F32) + dx).astype(BF16)

    waited = []

    def begin(name):
        slots = [0, 1, 2, 3] if PARTS[name] == 0 else [0, 1, 4, 5]
        for slot in slots[1:]:
            if slot % 2 and slot not in waited:
                waited.append(slot)
                nt_copies[slot].wait_recv()
        for copy in held_copies[name]:
            copy.wait_recv()
        order = [slots[0], slots[2], slots[1], slots[3]]
        lhs = jnp.concatenate([nt[slot] for slot in order], axis=1)
        chunks[name].begin(lhs, held[names.index(name)].reshape(4 * length, block))

    started = []

    def step(name):
        if name == "out":
            return begin_out()
        if name in PARTS and name not in started:
            started.append(name)
            begin(name)
            flight.append(name)
            return
        flight.remove(name)
        if not chunks[name].advance():
            flight.append(name)

    for name in DRAIN:
        step(name)
    for name in names:
        if name not in started:
            step(name)
    while flight:
        step(flight[0])
    home_copy.wait_recv()
    out_ref[0] = jnp.where(flag == 1, arrived[...].astype(F32), home[...].astype(F32)).astype(BF16)
    for copy in links.open:
        copy.wait_send()


def kernel(plan, scale, *refs):
    (lengths_hbm, swaps_hbm, x_hbm, up_hbm, win_hbm, wout_hbm, out_ref, dx_ref, diw_ref, dow_ref) = refs[:10]
    (win, wout, act, slope, weights, wslope, nt, nt_peer, gt, gt_peer, masked, masked_peer,
     hg_gate, hg_gate_peer, hg_pair, hg_pair_peer, home, arrived) = refs[10:28]
    lengths, swaps, x_ref, up_ref, load_sem, send_sem, recv_sem = refs[28:35]
    refs = list(refs[35:])
    length, width = plan.length, plan.width
    pair, pairs = 2 * HEAD_DIM, plan.pairs
    links = Links(plan, send_sem, recv_sem)

    barrier = pltpu.get_barrier_semaphore()
    friends = [links.sibling()]
    friends += [links.partner(flipped) for flipped in plan.masks()]
    for friend in friends:
        pl.semaphore_signal(barrier, inc=1, device_id=friend, device_id_type=MESH)
    moves = [(x_hbm, x_ref), (lengths_hbm, lengths), (up_hbm, up_ref), (swaps_hbm, swaps)]
    for j in range(4):
        columns = pl.ds(j * width, width)
        moves.append((win_hbm.at[:, columns], win.at[:, columns]))
    moves.append((wout_hbm, wout))
    loads = [pltpu.make_async_copy(a, b, load_sem.at[i]) for i, (a, b) in enumerate(moves)]
    for load in loads:
        load.start()
    for load in loads[:4]:
        load.wait()
    loads = loads[4:]

    live_count = lengths[0, links.w]
    flag = swaps[0, lax.rem(links.w, plan.shards // 2)]
    low = lax.broadcasted_iota(jnp.int32, (length, pair), 1) < HEAD_DIM
    query_at = lax.broadcasted_iota(jnp.int32, (length, length), 0)
    key_at = lax.broadcasted_iota(jnp.int32, (length, length), 1)
    allowed = (query_at >= key_at) & (key_at < live_count)
    allowed = jnp.concatenate([allowed, allowed], axis=0)

    def split_rows(values, target):
        across = values.astype(F32).T
        for w in range(plan.shards):
            core, z = w % 2, w // 2
            for q in range(plan.pieces):
                row = w * plan.share + q * plan.unit
                target[core, z * plan.pieces + q] = across[row : row + plan.unit].astype(BF16)

    def both(own, peer):
        mine = own[pl.ds(links.core, 1)].reshape(width // 2, length)
        return jnp.concatenate([mine, peer[...].reshape(width // 2, length)], axis=1)

    x = x_ref[0].astype(F32)
    x_scale = lax.rsqrt(jnp.mean(x * x, axis=-1, keepdims=True) + EPSILON)
    normed = (x * x_scale).astype(BF16)
    row_at = lax.broadcasted_iota(jnp.int32, (length, width), 0)
    masked[...] = jnp.where(row_at < live_count, up_ref[0].astype(F32), 0.0).astype(BF16)
    split_rows(normed, nt)
    pl.semaphore_wait(barrier, len(friends))
    masked_copy = links.send(masked, masked_peer, links.sibling())
    nt_copy = links.send(nt.at[1 - links.core], nt_peer, links.sibling())
    for j in range(4):
        loads[j].wait()
        columns = slice(j * width, (j + 1) * width)
        a, s = silu_and_slope(dot(normed, win[:, columns]))
        act[:, columns] = a.astype(BF16)
        slope[:, columns] = s

    def part(j, p):
        start = j * width + p * pair
        return act[:, start : start + pair]

    attended = []
    for p in range(pairs):
        scores = dot(stack_heads(part(2, p), low), part(3, p), 1, 1) * HEAD_DIM ** (-0.5)
        a, s = silu_and_slope(scores)
        a = jnp.where(allowed, a, 0.0).astype(BF16)
        weights[p] = a
        wslope[p] = jnp.where(allowed, s, 0.0) * HEAD_DIM ** (-0.5)
        attended.append(dot(side_by_side(a), stack_heads(part(1, p), low)))
    attended = jnp.concatenate(attended, axis=1)
    att_scale = lax.rsqrt(jnp.mean(attended * attended, axis=-1, keepdims=True) + EPSILON)
    gate = act[:, :width].astype(F32)
    att_normed = attended * att_scale
    gated = (gate * att_normed).astype(BF16)
    split_rows(gated, gt)
    gt_copy = links.send(gt.at[1 - links.core], gt_peer, links.sibling())
    loads[4].wait()
    home[...] = (x + dot(gated, wout[...])).astype(BF16)
    home_copy = links.send(home, arrived, links.partner([("z", plan.z_bits - 1)]))

    gated_grad = dot(masked[...], wout[...], 1, 1).astype(BF16).astype(F32)
    gate_grad = (gated_grad * att_normed).astype(BF16).astype(F32)
    hg_gate[...] = (gate_grad * slope[:, :width]).astype(BF16)
    hg_gate_copy = links.send(hg_gate, hg_gate_peer, links.sibling())
    norm_grad = gated_grad * gate
    along = jnp.mean(norm_grad * attended, axis=-1, keepdims=True)
    att_grad = (att_scale * norm_grad - attended * (att_scale * att_scale * att_scale * along)).astype(BF16)

    chunks, flight = {}, []

    def writer(name):
        kind, i = name.rstrip("0123456789"), int(name[-1])
        half = width // 2

        def write(values):
            values = values * scale
            if kind == "out":
                dow_ref[:, i * half : (i + 1) * half] = values
            elif kind == "gate":
                diw_ref[:, i * half : (i + 1) * half] = values
            else:
                for j in range(3):
                    start = (j + 1) * width + i * pair
                    diw_ref[:, start : start + pair] = values[:, j * pair : (j + 1) * pair]

        return write

    for spec in plan.chunks:
        n = len(plan.scratch_of(*spec))
        chunks[spec[0]] = Chunk(plan, links, spec, refs[:n], writer(spec[0]))
        refs = refs[n:]

    def begin(name, lhs, rhs):
        chunks[name].begin(lhs, rhs)
        flight.append(chunks[name])

    def advance(count):
        for _ in range(min(count, len(flight))):
            chunk = flight.pop(0)
            if not chunk.advance():
                flight.append(chunk)

    masked_copy.wait_recv()
    gt_copy.wait_recv()
    lhs = both(gt, gt_peer)
    for i in range(2):
        columns = slice(i * (width // 2), (i + 1) * (width // 2))
        begin("out%d" % i, lhs, jnp.concatenate([masked[:, columns], masked_peer[:, columns]], axis=0))

    pair_copies = []

    def pair_backward(p):
        q, k, v = part(2, p), part(3, p), part(1, p)
        q2 = stack_heads(q, low)
        da2 = stack_heads(att_grad[:, p * pair : (p + 1) * pair], low)
        weight_grad = dot(da2, v, 1, 1).astype(BF16).astype(F32)
        score_grad = (weight_grad * wslope[p]).astype(BF16)
        dv = dot(weights[p], da2, 0, 0)
        dq = dot(side_by_side(score_grad), stack_heads(k, low))
        dk = dot(score_grad, q2, 0, 0)
        for j, grad in enumerate((dv, dq, dk)):
            start = (j + 1) * width + p * pair
            grad = grad.astype(BF16).astype(F32) * slope[:, start : start + pair]
            hg_pair[p, :, j * pair : (j + 1) * pair] = grad.astype(BF16)
        pair_copies.append(links.send(hg_pair.at[p], hg_pair_peer.at[p], links.sibling()))

    def begin_pair(p):
        pair_copies[p].wait_recv()
        begin("pair%d" % p, lhs_in, jnp.concatenate([hg_pair[p], hg_pair_peer[p]], axis=0))

    pair_backward(0)
    hg_gate_copy.wait_recv()
    nt_copy.wait_recv()
    lhs_in = both(nt, nt_peer)
    for i in range(2):
        columns = slice(i * (width // 2), (i + 1) * (width // 2))
        begin("gate%d" % i, lhs_in, jnp.concatenate([hg_gate[:, columns], hg_gate_peer[:, columns]], axis=0))
    for p in range(1, pairs):
        pair_backward(p)
        begin_pair(p - 1)

    back = dot(hg_gate[...], win[:, :width], 1, 1)
    for p in range(pairs):
        if p == 1:
            begin_pair(pairs - 1)
        for j in range(3):
            start = (j + 1) * width + p * pair
            back += dot(hg_pair[p, :, j * pair : (j + 1) * pair], win[:, start : start + pair], 1, 1)
    along = jnp.mean(back * x, axis=-1, keepdims=True)
    dx = x_scale * back - x * (x_scale * x_scale * x_scale * along)
    dx_ref[0] = (masked[...].astype(F32) + dx).astype(BF16)

    while flight:
        advance(1)
    home_copy.wait_recv()
    out_ref[0] = jnp.where(flag == 1, arrived[...].astype(F32), home[...].astype(F32)).astype(BF16)
    for copy in links.open:
        copy.wait_send()


def store_kernel(*refs):
    sems = refs[8]
    copies = [pltpu.make_async_copy(refs[i], refs[4 + i], sems.at[i]) for i in range(4)]
    for copy in copies:
        copy.start()
    for copy in copies:
        copy.wait()


def body(plan, sequences, upstream, lengths, swap_table, input_weight, output_weight):
    length, width = plan.length, plan.width
    scale = 1.0 / math.sqrt(length * plan.shards * plan.groups)
    rows = plan.units, plan.unit, length
    pair, pairs = 2 * HEAD_DIM, plan.pairs
    vmem = lambda *shape: pltpu.VMEM(shape, BF16)
    quad = isinstance(plan, QuadPlan)
    if quad:
        exchanged = [
            vmem(6, width, length),
            vmem(2, *rows),
            vmem(*rows),
            vmem(length, width),
            vmem(length, width),
            vmem(4, 4, length, plan.block),
            vmem(4, 4, length, plan.block),
        ]
    else:
        exchanged = [
            vmem(2, *rows),
            vmem(*rows),
            vmem(2, *rows),
            vmem(*rows),
            vmem(length, width),
            vmem(length, width),
            vmem(length, width),
            vmem(length, width),
            vmem(pairs, length, 3 * pair),
            vmem(pairs, length, 3 * pair),
        ]
    scratch = [
        vmem(width, 4 * width),
        vmem(width, width),
        vmem(length, 4 * width),
        pltpu.VMEM((length, 4 * width), F32),
        vmem(pairs, 2 * length, length),
        pltpu.VMEM((pairs, 2 * length, length), F32),
        *exchanged,
        vmem(length, width),
        vmem(length, width),
        pltpu.SMEM((1, plan.shards), jnp.int32),
        pltpu.SMEM((1, plan.shards // 2), jnp.int32),
        vmem(1, length, width),
        vmem(1, length, width),
        pltpu.SemaphoreType.DMA((9,)),
        pltpu.SemaphoreType.DMA((plan.copies(),)),
        pltpu.SemaphoreType.DMA((plan.copies(),)),
    ]
    for spec in plan.chunks:
        scratch += [vmem(*shape) for shape in plan.scratch_of(*spec)]
    for name in PARTS if quad else ():
        scratch += [vmem(*shape) for shape in plan.part_scratch(name)]
    in_vmem = pl.BlockSpec(memory_space=pltpu.VMEM)
    in_hbm = pl.BlockSpec(memory_space=pltpu.HBM)
    results = pl.pallas_call(
        functools.partial(quad_kernel if quad else kernel, plan, scale),
        out_shape=(
            pltpu.VMEM(sequences.shape, BF16),
            pltpu.VMEM(sequences.shape, BF16),
            pltpu.VMEM((plan.share, 4 * width), F32),
            pltpu.VMEM((plan.share, width), F32),
        ),
        in_specs=[in_hbm] * 6,
        out_specs=(in_vmem,) * 4,
        scratch_shapes=scratch,
        compiler_params=pltpu.CompilerParams(
            collective_id=0, has_side_effects=True, vmem_limit_bytes=LIMIT
        ),
    )(lengths[:, :, 0], swap_table[:, :, 0], sequences, upstream, input_weight, output_weight)
    return pl.pallas_call(
        store_kernel,
        out_shape=tuple(jax.ShapeDtypeStruct(r.shape, r.dtype) for r in results),
        in_specs=[pl.BlockSpec(memory_space=pl.ANY)] * 4,
        out_specs=(in_hbm,) * 4,
        scratch_shapes=[pltpu.SemaphoreType.DMA((4,))],
        compiler_params=pltpu.CompilerParams(vmem_limit_bytes=8 * 1024 * 1024),
    )(*results)


def solution(mesh):
    groups, shards = mesh.shape["grp"], mesh.shape["wide"]
    split = P(("grp", "wide"), None, None)

    def whole(sequences, upstream, lengths, swap_table, input_weight, output_weight):
        sizes = groups, shards, sequences.shape[1], sequences.shape[2]
        plan = QuadPlan(*sizes) if QuadPlan.fits(*sizes) else Plan(*sizes)
        return jax.shard_map(
            functools.partial(body, plan),
            mesh=mesh,
            in_specs=(split, split, P("grp", None, None), P("grp", None, None), P(), P()),
            out_specs=(split, split, P("wide", None), P("wide", None)),
            check_vma=False,
        )(sequences, upstream, lengths, swap_table, input_weight, output_weight)

    return whole
```

```python
import functools
import math

import jax
import jax.numpy as jnp
from jax import lax
from jax.experimental import pallas as pl
from jax.experimental.pallas import tpu as pltpu
from jax.sharding import PartitionSpec as P

HEADS = 8
HEAD_DIM = 64
EPSILON = 1e-06
MODES = {'out0': 'g01,z01,G', 'out1': 'g01,z01,G'}
PARTS = {"gate": 0, "value": 1, "query": 0, "key": 1}
PART_Z = {'gate': '01', 'value': 's,01', 'query': 's,01', 'key': 's,01'}
DRAIN = ('out', 'gate', 'value', 'query', 'key', 'out0', 'out1', 'value', 'gate', 'query', 'key', 'out0', 'out1', 'value', 'query', 'key')
OUT_AT = 2
LIMIT = 67043328 - 1024 * 1024
MESH = pl.DeviceIdType.MESH
F32 = jnp.float32
BF16 = jnp.bfloat16


def dot(a, b, ca=1, cb=0):
    return lax.dot_general(a, b, (((ca,), (cb,)), ((), ())), preferred_element_type=F32)


def silu_and_slope(h):
    s = 0.5 * jnp.tanh(0.5 * h) + 0.5
    a = h * s
    return a, s + a * (1.0 - s)


def stack_heads(a, low):
    zero = jnp.zeros_like(a)
    return jnp.concatenate([jnp.where(low, a, zero), jnp.where(low, zero, a)], axis=0)


def side_by_side(a):
    half = a.shape[0] // 2
    return jnp.concatenate([a[:half], a[half:]], axis=1)


def bits_of(n):
    return n.bit_length() - 1


class Plan:
    def __init__(self, groups, shards, length, width):
        self.groups, self.shards, self.length, self.width = groups, shards, length, width
        self.chips = shards // 2
        self.share = width // shards
        self.unit = min(16, self.share)
        self.pieces = min(self.share // self.unit, groups)
        self.unit = self.share // self.pieces
        self.units = self.pieces * self.chips
        self.grp_bits = bits_of(groups)
        self.z_bits = bits_of(self.chips)
        self.q_bits = bits_of(self.pieces)
        pair = 2 * HEAD_DIM
        self.pairs = width // pair
        half = width // 2
        self.chunks = [("out%d" % i, half) for i in range(2)]
        self.chunks += [("gate%d" % i, half) for i in range(2)]
        self.chunks += [("pair%d" % p, 3 * pair) for p in range(self.pairs)]

    def stages(self, name):
        g_bits = [("g", b) for b in range(self.grp_bits)]
        z_bits = [("z", b) for b in range(self.z_bits)]
        if name not in MODES or self.q_bits != 2 or self.grp_bits != 2 or self.z_bits != 2:
            halve, rest = g_bits[: self.q_bits], g_bits[self.q_bits :]
            found = [("split", [b]) for b in halve + z_bits] + [("add", [b]) for b in rest]
            return found + ([("gather", halve)] if halve else [])
        found, halved = [], []
        for word in MODES[name].split(","):
            kind = {"g": "split", "z": "split", "a": "add", "G": "gather"}[word[0]]
            bits = [("z" if word[0] == "z" else "g", int(b)) for b in word[1:]]
            if word[0] == "g":
                halved += bits
            found.append((kind, halved if kind == "gather" else bits))
        return found

    def unit_order(self, name):
        bits = [b for kind, bits in self.stages(name) if kind == "split" for b in bits]
        whole = [("g", b) for b in range(self.q_bits) if ("g", b) not in bits]
        bits = bits + whole
        order = []
        for u in range(self.units):
            z = q = 0
            for i, (axis, b) in enumerate(bits):
                bit = (u >> (len(bits) - 1 - i)) % 2
                if axis == "z":
                    z += bit << b
                else:
                    q = q * 2 + bit
            order.append(z * self.pieces + q)
        return order

    def scratch_of(self, name, columns):
        shapes, units = [(self.units, self.unit, columns)], self.units
        for kind, bits in self.stages(name):
            if kind == "split":
                units >>= len(bits)
            if kind != "gather":
                shapes.append(((2 ** len(bits) - 1) * units, self.unit, columns))
                shapes.append((units, self.unit, columns))
            else:
                shapes.append((self.pieces, self.unit, columns))
        return shapes

    def copies(self):
        n = 5 + self.pairs
        for name, _ in self.chunks:
            for kind, bits in self.stages(name):
                n += 2 ** len(bits) - 1
        return n

    def masks(self):
        found = []
        for name, _ in self.chunks:
            for kind, bits in self.stages(name):
                for flipped in flips(bits):
                    if sorted(flipped) not in found:
                        found.append(sorted(flipped))
        top = [("z", self.z_bits - 1)]
        return found if top in found else found + [top]


def flips(bits):
    return [
        [b for i, b in enumerate(bits) if (m >> i) % 2] for m in range(1, 2 ** len(bits))
    ]


class Links:
    def __init__(self, plan, send_sem, recv_sem):
        self.send_sem, self.recv_sem, self.count, self.open = send_sem, recv_sem, 0, []
        self.g, self.w = lax.axis_index("grp"), lax.axis_index("wide")
        self.core = lax.rem(self.w, 2)
        self.z = lax.div(self.w, 2)

    def bit(self, which):
        axis, b = which
        if axis == "c":
            return self.core
        return lax.rem(lax.div(self.g if axis == "g" else self.z, 1 << b), 2)

    def partner(self, flipped):
        g, w = self.g, self.w
        for axis, b in flipped:
            step = (1 << b) * (1 - 2 * self.bit((axis, b)))
            if axis == "g":
                g = g + step
            else:
                w = w + (step if axis == "c" else 2 * step)
        return (g, w)

    def place(self, bits, flipped=()):
        at = 0
        for which in bits:
            bit = self.bit(which)
            at = at * 2 + (1 - bit if which in flipped else bit)
        return at

    def sibling(self):
        return (self.g, self.w + 1 - 2 * self.core)

    def send(self, source, target, device):
        i = self.count
        self.count += 1
        copy = pltpu.make_async_remote_copy(
            src_ref=source,
            dst_ref=target,
            send_sem=self.send_sem.at[i],
            recv_sem=self.recv_sem.at[i],
            device_id=device,
            device_id_type=MESH,
        )
        copy.start()
        self.open.append(copy)
        return copy


class Chunk:
    def __init__(self, plan, links, spec, refs, write):
        name, self.columns = spec
        self.plan, self.links, self.write = plan, links, write
        self.stages, self.order = plan.stages(name), plan.unit_order(name)
        refs = list(refs)
        self.now, self.rest = refs[0], refs[1:]
        self.units, self.step, self.copies = plan.units, 0, []

    def begin(self, lhs, rhs):
        u = self.plan.unit
        lhs = jnp.concatenate([lhs[i * u : (i + 1) * u] for i in self.order], axis=0)
        value = dot(lhs, rhs).astype(BF16)
        self.now[...] = value.reshape(self.now.shape)
        self.launch()

    def launch(self):
        kind, bits = self.stages[self.step]
        links, self.copies = self.links, []
        if kind == "gather":
            own = self.rest[0].at[pl.ds(links.place(bits), 1)]
            own[...] = self.now[...]
        for i, flipped in enumerate(flips(bits)):
            if kind == "split":
                size = self.units >> len(bits)
                source = self.now.at[pl.ds(links.place(bits, flipped) * size, size)]
                target = self.rest[0].at[pl.ds(i * size, size)]
            elif kind == "add":
                source, target = self.now, self.rest[0].at[pl.ds(i * self.units, self.units)]
            else:
                source, target = own, own
            self.copies.append(links.send(source, target, links.partner(flipped)))

    def advance(self):
        kind, bits = self.stages[self.step]
        for copy in self.copies:
            copy.wait_recv()
        if kind != "gather":
            if kind == "split":
                self.units >>= len(bits)
            size = self.units
            mine = self.links.place(bits) if kind == "split" else 0
            total = self.now[pl.ds(mine * size, size)].astype(F32)
            arrived, result = self.rest[:2]
            self.rest = self.rest[2:]
            for i in range(len(self.copies)):
                total += arrived[i * size : (i + 1) * size].astype(F32)
            result[...] = total.astype(BF16)
            self.now = result
        else:
            self.now = self.rest[0]
        self.step += 1
        if self.step < len(self.stages):
            self.launch()
            return False
        self.write(self.now[...].astype(F32).reshape(self.plan.share, self.columns))
        return True


CORE = ("c", 0)


class QuadPlan(Plan):
    def __init__(self, *sizes):
        super().__init__(*sizes)
        self.chunks = self.chunks[:2]
        self.block = self.width // 4
        self.piece = self.share // 2

    @staticmethod
    def fits(groups, shards, length, width):
        return groups == 4 and shards == 8 and width % 512 == 0 and length % 128 == 0

    def quad(self, name):
        return [("g", PARTS[name]), CORE]

    def part_stages(self, name):
        across = ("g", 1 - PARTS[name])
        named = {"s": across, "0": ("z", 0), "1": ("z", 1)}
        words = [[named[letter] for letter in word] for word in PART_Z[name].split(",")]
        last = "spread" if self.halved(name) else "share"
        return [("split", bits) for bits in words] + [(last, [across] + self.quad(name))]

    @staticmethod
    def halved(name):
        return "s" in PART_Z[name]

    def part_order(self, name):
        units = range(4 * self.chips)
        if self.halved(name):
            return units
        return [u % 2 * 2 * self.chips + u // 4 * 2 + u // 2 % 2 for u in units]

    def rows_of_units(self):
        rows = []
        for half in range(2):
            for at in range(self.chips):
                z = sum(((at >> (self.z_bits - 1 - b)) % 2) << b for b in range(self.z_bits))
                for core in range(2):
                    rows.append((2 * z + core) * self.share + half * self.piece)
        return rows

    def part_scratch(self, name):
        units = 4 * self.chips
        shapes = [(units, self.piece, self.block)]
        for kind, bits in self.part_stages(name):
            if kind == "split":
                units >>= len(bits)
                shapes.append(((2 ** len(bits) - 1) * units, self.piece, self.block))
                shapes.append((units, self.piece, self.block))
            else:
                shapes.append((8 * (1 if kind == "spread" else 2), self.piece, self.block))
        return shapes

    def copies(self):
        n = super().copies() - 5 - self.pairs + 8 + 3 * len(PARTS)
        for name in PARTS:
            n += sum(2 ** len(bits) - 1 for _, bits in self.part_stages(name))
        return n

    def masks(self):
        found = super().masks()
        for name in PARTS:
            for _, bits in self.part_stages(name):
                for flipped in flips(bits):
                    if sorted(flipped) not in found:
                        found.append(sorted(flipped))
        return [m for m in found if m != [CORE]]


class Part(Chunk):
    def __init__(self, plan, links, name, refs, write):
        self.plan, self.links, self.write, self.name = plan, links, write, name
        self.columns, self.stages = plan.block, plan.part_stages(name)
        self.now, self.rest = refs[0], list(refs[1:])
        self.units, self.step, self.copies = 4 * plan.chips, 0, []

    def begin(self, lhs, rhs):
        value = dot(lhs, rhs).astype(BF16).reshape(self.now.shape)
        for i, u in enumerate(self.plan.part_order(self.name)):
            self.now[i] = value[u]
        self.launch()

    def launch(self):
        kind, bits = self.stages[self.step]
        if kind == "split":
            return super().launch()
        links, self.copies, all_of = self.links, [], self.rest[0]
        size = 1 if kind == "spread" else 2
        own = all_of.at[pl.ds(links.place(bits) * size, size)]
        own[...] = self.now[pl.ds(links.core * size, size)]
        for flipped in flips(bits):
            core = 1 - links.core if CORE in flipped else links.core
            source = self.now.at[pl.ds(core * size, size)]
            self.copies.append(links.send(source, own, links.partner(flipped)))

    def advance(self):
        if self.stages[self.step][0] == "split":
            return super().advance()
        for copy in self.copies:
            copy.wait_recv()
        self.write(self.rest[0])
        return True


def quad_kernel(plan, scale, *refs):
    (lengths_hbm, swaps_hbm, x_hbm, up_hbm, win_hbm, wout_hbm, out_ref, dx_ref, diw_ref, dow_ref) = refs[:10]
    (win, wout, act, slope, weights, wslope, nt, gt, gt_peer, masked, masked_peer,
     blocks, held, home, arrived) = refs[10:25]
    lengths, swaps, x_ref, up_ref, load_sem, send_sem, recv_sem = refs[25:32]
    refs = list(refs[32:])
    length, width, block = plan.length, plan.width, plan.block
    pair, pairs = 2 * HEAD_DIM, plan.pairs
    links = Links(plan, send_sem, recv_sem)
    names = list(PARTS)

    barrier = pltpu.get_barrier_semaphore()
    friends = [links.sibling()]
    friends += [links.partner(flipped) for flipped in plan.masks()]
    for friend in friends:
        pl.semaphore_signal(barrier, inc=1, device_id=friend, device_id_type=MESH)
    moves = [(x_hbm, x_ref), (lengths_hbm, lengths), (up_hbm, up_ref), (swaps_hbm, swaps)]
    for j in range(4):
        columns = pl.ds(j * width, width)
        moves.append((win_hbm.at[:, columns], win.at[:, columns]))
    moves.append((wout_hbm, wout))
    loads = [pltpu.make_async_copy(a, b, load_sem.at[i]) for i, (a, b) in enumerate(moves)]
    for load in loads:
        load.start()
    loads[0].wait()

    x = x_ref[0].astype(F32)
    x_scale = lax.rsqrt(jnp.mean(x * x, axis=-1, keepdims=True) + EPSILON)
    normed = (x * x_scale).astype(BF16)
    across = (x * x_scale).astype(BF16).astype(F32).T
    piece = plan.piece
    for i, row in enumerate(plan.rows_of_units()):
        nt[0, i * piece : (i + 1) * piece] = across[row : row + piece].astype(BF16)
    pl.semaphore_wait(barrier, len(friends))
    nt_copies = {}
    for slot, flipped in ((2, [("g", 0)]), (4, [("g", 1)]), (1, [CORE])):
        nt_copies[slot] = links.send(nt.at[0], nt.at[slot], links.partner(flipped))
    for load in loads[1:4]:
        load.wait()
    loads = loads[4:]
    live_count = lengths[0, links.w]
    flag = swaps[0, lax.rem(links.w, plan.shards // 2)]
    low = lax.broadcasted_iota(jnp.int32, (length, pair), 1) < HEAD_DIM
    query_at = lax.broadcasted_iota(jnp.int32, (length, length), 0)
    key_at = lax.broadcasted_iota(jnp.int32, (length, length), 1)
    allowed = (query_at >= key_at) & (key_at < live_count)
    allowed = jnp.concatenate([allowed, allowed], axis=0)

    row_at = lax.broadcasted_iota(jnp.int32, (length, width), 0)
    masked[...] = jnp.where(row_at < live_count, up_ref[0].astype(F32), 0.0).astype(BF16)
    masked_copy = links.send(masked, masked_peer, links.sibling())
    for j in range(4):
        loads[j].wait()
        columns = slice(j * width, (j + 1) * width)
        a, s = silu_and_slope(dot(normed, win[:, columns]))
        act[:, columns] = a.astype(BF16)
        slope[:, columns] = s

    def part(j, p):
        start = j * width + p * pair
        return act[:, start : start + pair]

    attended = []
    for p in range(pairs):
        scores = dot(stack_heads(part(2, p), low), part(3, p), 1, 1) * HEAD_DIM ** (-0.5)
        a, s = silu_and_slope(scores)
        a = jnp.where(allowed, a, 0.0).astype(BF16)
        weights[p] = a
        wslope[p] = jnp.where(allowed, s, 0.0) * HEAD_DIM ** (-0.5)
        attended.append(dot(side_by_side(a), stack_heads(part(1, p), low)))
    attended = jnp.concatenate(attended, axis=1)
    att_scale = lax.rsqrt(jnp.mean(attended * attended, axis=-1, keepdims=True) + EPSILON)
    gate = act[:, :width].astype(F32)
    att_normed = attended * att_scale
    gated = (gate * att_normed).astype(BF16)
    turned = gated.astype(F32).T
    for w in range(plan.shards):
        core, z = w % 2, w // 2
        for q in range(plan.pieces):
            row = w * plan.share + q * plan.unit
            gt[core, z * plan.pieces + q] = turned[row : row + plan.unit].astype(BF16)
    gt_copy = links.send(gt.at[1 - links.core], gt_peer, links.sibling())
    loads[4].wait()
    home[...] = (x + dot(gated, wout[...])).astype(BF16)
    home_copy = links.send(home, arrived, links.partner([("z", plan.z_bits - 1)]))

    gated_grad = dot(masked[...], wout[...], 1, 1).astype(BF16).astype(F32)
    gate_grad = (gated_grad * att_normed).astype(BF16).astype(F32)
    hg = (gate_grad * slope[:, :width]).astype(BF16)

    held_copies = {}

    def offer(name):
        j, quad = names.index(name), plan.quad(name)
        held[j, 0:1] = blocks[j, pl.ds(links.place(quad), 1)]
        copies = []
        for i, flipped in enumerate(flips(quad)):
            source = blocks.at[j, pl.ds(links.place(quad, flipped), 1)]
            target = held.at[j, pl.ds(i + 1, 1)]
            copies.append(links.send(source, target, links.partner(flipped)))
        held_copies[name] = copies

    for b in range(4):
        blocks[0, b] = hg[:, b * block : (b + 1) * block]
    offer("gate")
    norm_grad = gated_grad * gate
    along = jnp.mean(norm_grad * attended, axis=-1, keepdims=True)
    att_grad = (att_scale * norm_grad - attended * (att_scale * att_scale * att_scale * along)).astype(BF16)
    both_heads = [stack_heads(att_grad[:, p * pair : (p + 1) * pair], low) for p in range(pairs)]

    def put(j, p, grad):
        start = j * width + p * pair
        grad = (grad.astype(BF16).astype(F32) * slope[:, start : start + pair]).astype(BF16)
        blocks[j, p] = grad

    for p in range(pairs):
        put(1, p, dot(weights[p], both_heads[p], 0, 0))
    offer("value")

    chunks, flight, lines = {}, [], plan.piece

    def out_writer(i):
        half = width // 2

        def write(values):
            dow_ref[:, i * half : (i + 1) * half] = values * scale

        return write

    def part_writer(name):
        j = names.index(name)

        def write(ref):
            for m in range(8):
                row, column = (m // 4) * lines, j * width + (m % 4) * block
                if plan.halved(name):
                    total = ref[m].astype(F32)
                else:
                    i = (m % 4) * 2 + m // 4
                    total = ref[i].astype(F32) + ref[i + 8].astype(F32)
                diw_ref[row : row + lines, column : column + block] = total * scale

        return write

    for i, spec in enumerate(plan.chunks):
        n = len(plan.scratch_of(*spec))
        chunks[spec[0]] = Chunk(plan, links, spec, refs[:n], out_writer(i))
        refs = refs[n:]
    for name in names:
        n = len(plan.part_scratch(name))
        chunks[name] = Part(plan, links, name, refs[:n], part_writer(name))
        refs = refs[n:]

    def begin_out():
        masked_copy.wait_recv()
        gt_copy.wait_recv()
        mine = gt[pl.ds(links.core, 1)].reshape(width // 2, length)
        lhs = jnp.concatenate([mine, gt_peer[...].reshape(width // 2, length)], axis=1)
        for i in range(2):
            columns = slice(i * (width // 2), (i + 1) * (width // 2))
            chunks["out%d" % i].begin(lhs, jnp.concatenate([masked[:, columns], masked_peer[:, columns]], axis=0))
            flight.append("out%d" % i)

    if OUT_AT == 0:
        begin_out()
    score_grads = []
    for p in range(pairs):
        weight_grad = dot(both_heads[p], part(1, p), 1, 1).astype(BF16).astype(F32)
        score_grads.append((weight_grad * wslope[p]).astype(BF16))
        put(2, p, dot(side_by_side(score_grads[p]), stack_heads(part(3, p), low)))
    offer("query")
    for p in range(pairs):
        put(3, p, dot(score_grads[p], stack_heads(part(2, p), low), 0, 0))
    offer("key")

    if OUT_AT == 1:
        begin_out()
    for slot in (2, 4):
        nt_copies[slot].wait_recv()
        nt_copies[slot + 1] = links.send(nt.at[slot], nt.at[slot + 1], links.sibling())

    back = 0.0
    for j in range(4):
        grads = jnp.concatenate([blocks[j, b] for b in range(4)], axis=1)
        back += dot(grads, win[:, j * width : (j + 1) * width], 1, 1)
    along = jnp.mean(back * x, axis=-1, keepdims=True)
    dx = x_scale * back - x * (x_scale * x_scale * x_scale * along)
    dx_ref[0] = (masked[...].astype(F32) + dx).astype(BF16)

    waited = []

    def begin(name):
        slots = [0, 1, 2, 3] if PARTS[name] == 0 else [0, 1, 4, 5]
        for slot in slots[1:]:
            if slot % 2 and slot not in waited:
                waited.append(slot)
                nt_copies[slot].wait_recv()
        for copy in held_copies[name]:
            copy.wait_recv()
        order = [slots[0], slots[2], slots[1], slots[3]]
        lhs = jnp.concatenate([nt[slot] for slot in order], axis=1)
        chunks[name].begin(lhs, held[names.index(name)].reshape(4 * length, block))

    started = []

    def step(name):
        if name == "out":
            return begin_out()
        if name in PARTS and name not in started:
            started.append(name)
            begin(name)
            flight.append(name)
            return
        flight.remove(name)
        if not chunks[name].advance():
            flight.append(name)

    for name in DRAIN:
        step(name)
    for name in names:
        if name not in started:
            step(name)
    while flight:
        step(flight[0])
    home_copy.wait_recv()
    out_ref[0] = jnp.where(flag == 1, arrived[...].astype(F32), home[...].astype(F32)).astype(BF16)
    for copy in links.open:
        copy.wait_send()


def kernel(plan, scale, *refs):
    (lengths_hbm, swaps_hbm, x_hbm, up_hbm, win_hbm, wout_hbm, out_ref, dx_ref, diw_ref, dow_ref) = refs[:10]
    (win, wout, act, slope, weights, wslope, nt, nt_peer, gt, gt_peer, masked, masked_peer,
     hg_gate, hg_gate_peer, hg_pair, hg_pair_peer, home, arrived) = refs[10:28]
    lengths, swaps, x_ref, up_ref, load_sem, send_sem, recv_sem = refs[28:35]
    refs = list(refs[35:])
    length, width = plan.length, plan.width
    pair, pairs = 2 * HEAD_DIM, plan.pairs
    links = Links(plan, send_sem, recv_sem)

    barrier = pltpu.get_barrier_semaphore()
    friends = [links.sibling()]
    friends += [links.partner(flipped) for flipped in plan.masks()]
    for friend in friends:
        pl.semaphore_signal(barrier, inc=1, device_id=friend, device_id_type=MESH)
    moves = [(x_hbm, x_ref), (lengths_hbm, lengths), (up_hbm, up_ref), (swaps_hbm, swaps)]
    for j in range(4):
        columns = pl.ds(j * width, width)
        moves.append((win_hbm.at[:, columns], win.at[:, columns]))
    moves.append((wout_hbm, wout))
    loads = [pltpu.make_async_copy(a, b, load_sem.at[i]) for i, (a, b) in enumerate(moves)]
    for load in loads:
        load.start()
    for load in loads[:4]:
        load.wait()
    loads = loads[4:]

    live_count = lengths[0, links.w]
    flag = swaps[0, lax.rem(links.w, plan.shards // 2)]
    low = lax.broadcasted_iota(jnp.int32, (length, pair), 1) < HEAD_DIM
    query_at = lax.broadcasted_iota(jnp.int32, (length, length), 0)
    key_at = lax.broadcasted_iota(jnp.int32, (length, length), 1)
    allowed = (query_at >= key_at) & (key_at < live_count)
    allowed = jnp.concatenate([allowed, allowed], axis=0)

    def split_rows(values, target):
        across = values.astype(F32).T
        for w in range(plan.shards):
            core, z = w % 2, w // 2
            for q in range(plan.pieces):
                row = w * plan.share + q * plan.unit
                target[core, z * plan.pieces + q] = across[row : row + plan.unit].astype(BF16)

    def both(own, peer):
        mine = own[pl.ds(links.core, 1)].reshape(width // 2, length)
        return jnp.concatenate([mine, peer[...].reshape(width // 2, length)], axis=1)

    x = x_ref[0].astype(F32)
    x_scale = lax.rsqrt(jnp.mean(x * x, axis=-1, keepdims=True) + EPSILON)
    normed = (x * x_scale).astype(BF16)
    row_at = lax.broadcasted_iota(jnp.int32, (length, width), 0)
    masked[...] = jnp.where(row_at < live_count, up_ref[0].astype(F32), 0.0).astype(BF16)
    split_rows(normed, nt)
    pl.semaphore_wait(barrier, len(friends))
    masked_copy = links.send(masked, masked_peer, links.sibling())
    nt_copy = links.send(nt.at[1 - links.core], nt_peer, links.sibling())
    for j in range(4):
        loads[j].wait()
        columns = slice(j * width, (j + 1) * width)
        a, s = silu_and_slope(dot(normed, win[:, columns]))
        act[:, columns] = a.astype(BF16)
        slope[:, columns] = s

    def part(j, p):
        start = j * width + p * pair
        return act[:, start : start + pair]

    attended = []
    for p in range(pairs):
        scores = dot(stack_heads(part(2, p), low), part(3, p), 1, 1) * HEAD_DIM ** (-0.5)
        a, s = silu_and_slope(scores)
        a = jnp.where(allowed, a, 0.0).astype(BF16)
        weights[p] = a
        wslope[p] = jnp.where(allowed, s, 0.0) * HEAD_DIM ** (-0.5)
        attended.append(dot(side_by_side(a), stack_heads(part(1, p), low)))
    attended = jnp.concatenate(attended, axis=1)
    att_scale = lax.rsqrt(jnp.mean(attended * attended, axis=-1, keepdims=True) + EPSILON)
    gate = act[:, :width].astype(F32)
    att_normed = attended * att_scale
    gated = (gate * att_normed).astype(BF16)
    split_rows(gated, gt)
    gt_copy = links.send(gt.at[1 - links.core], gt_peer, links.sibling())
    loads[4].wait()
    home[...] = (x + dot(gated, wout[...])).astype(BF16)
    home_copy = links.send(home, arrived, links.partner([("z", plan.z_bits - 1)]))

    gated_grad = dot(masked[...], wout[...], 1, 1).astype(BF16).astype(F32)
    gate_grad = (gated_grad * att_normed).astype(BF16).astype(F32)
    hg_gate[...] = (gate_grad * slope[:, :width]).astype(BF16)
    hg_gate_copy = links.send(hg_gate, hg_gate_peer, links.sibling())
    norm_grad = gated_grad * gate
    along = jnp.mean(norm_grad * attended, axis=-1, keepdims=True)
    att_grad = (att_scale * norm_grad - attended * (att_scale * att_scale * att_scale * along)).astype(BF16)

    chunks, flight = {}, []

    def writer(name):
        kind, i = name.rstrip("0123456789"), int(name[-1])
        half = width // 2

        def write(values):
            values = values * scale
            if kind == "out":
                dow_ref[:, i * half : (i + 1) * half] = values
            elif kind == "gate":
                diw_ref[:, i * half : (i + 1) * half] = values
            else:
                for j in range(3):
                    start = (j + 1) * width + i * pair
                    diw_ref[:, start : start + pair] = values[:, j * pair : (j + 1) * pair]

        return write

    for spec in plan.chunks:
        n = len(plan.scratch_of(*spec))
        chunks[spec[0]] = Chunk(plan, links, spec, refs[:n], writer(spec[0]))
        refs = refs[n:]

    def begin(name, lhs, rhs):
        chunks[name].begin(lhs, rhs)
        flight.append(chunks[name])

    def advance(count):
        for _ in range(min(count, len(flight))):
            chunk = flight.pop(0)
            if not chunk.advance():
                flight.append(chunk)

    masked_copy.wait_recv()
    gt_copy.wait_recv()
    lhs = both(gt, gt_peer)
    for i in range(2):
        columns = slice(i * (width // 2), (i + 1) * (width // 2))
        begin("out%d" % i, lhs, jnp.concatenate([masked[:, columns], masked_peer[:, columns]], axis=0))

    pair_copies = []

    def pair_backward(p):
        q, k, v = part(2, p), part(3, p), part(1, p)
        q2 = stack_heads(q, low)
        da2 = stack_heads(att_grad[:, p * pair : (p + 1) * pair], low)
        weight_grad = dot(da2, v, 1, 1).astype(BF16).astype(F32)
        score_grad = (weight_grad * wslope[p]).astype(BF16)
        dv = dot(weights[p], da2, 0, 0)
        dq = dot(side_by_side(score_grad), stack_heads(k, low))
        dk = dot(score_grad, q2, 0, 0)
        for j, grad in enumerate((dv, dq, dk)):
            start = (j + 1) * width + p * pair
            grad = grad.astype(BF16).astype(F32) * slope[:, start : start + pair]
            hg_pair[p, :, j * pair : (j + 1) * pair] = grad.astype(BF16)
        pair_copies.append(links.send(hg_pair.at[p], hg_pair_peer.at[p], links.sibling()))

    def begin_pair(p):
        pair_copies[p].wait_recv()
        begin("pair%d" % p, lhs_in, jnp.concatenate([hg_pair[p], hg_pair_peer[p]], axis=0))

    pair_backward(0)
    hg_gate_copy.wait_recv()
    nt_copy.wait_recv()
    lhs_in = both(nt, nt_peer)
    for i in range(2):
        columns = slice(i * (width // 2), (i + 1) * (width // 2))
        begin("gate%d" % i, lhs_in, jnp.concatenate([hg_gate[:, columns], hg_gate_peer[:, columns]], axis=0))
    for p in range(1, pairs):
        pair_backward(p)
        begin_pair(p - 1)

    back = dot(hg_gate[...], win[:, :width], 1, 1)
    for p in range(pairs):
        if p == 1:
            begin_pair(pairs - 1)
        for j in range(3):
            start = (j + 1) * width + p * pair
            back += dot(hg_pair[p, :, j * pair : (j + 1) * pair], win[:, start : start + pair], 1, 1)
    along = jnp.mean(back * x, axis=-1, keepdims=True)
    dx = x_scale * back - x * (x_scale * x_scale * x_scale * along)
    dx_ref[0] = (masked[...].astype(F32) + dx).astype(BF16)

    while flight:
        advance(1)
    home_copy.wait_recv()
    out_ref[0] = jnp.where(flag == 1, arrived[...].astype(F32), home[...].astype(F32)).astype(BF16)
    for copy in links.open:
        copy.wait_send()


def store_kernel(*refs):
    sems = refs[8]
    copies = [pltpu.make_async_copy(refs[i], refs[4 + i], sems.at[i]) for i in range(4)]
    for copy in copies:
        copy.start()
    for copy in copies:
        copy.wait()


def body(plan, sequences, upstream, lengths, swap_table, input_weight, output_weight):
    length, width = plan.length, plan.width
    scale = 1.0 / math.sqrt(length * plan.shards * plan.groups)
    rows = plan.units, plan.unit, length
    pair, pairs = 2 * HEAD_DIM, plan.pairs
    vmem = lambda *shape: pltpu.VMEM(shape, BF16)
    quad = isinstance(plan, QuadPlan)
    if quad:
        exchanged = [
            vmem(6, width, length),
            vmem(2, *rows),
            vmem(*rows),
            vmem(length, width),
            vmem(length, width),
            vmem(4, 4, length, plan.block),
            vmem(4, 4, length, plan.block),
        ]
    else:
        exchanged = [
            vmem(2, *rows),
            vmem(*rows),
            vmem(2, *rows),
            vmem(*rows),
            vmem(length, width),
            vmem(length, width),
            vmem(length, width),
            vmem(length, width),
            vmem(pairs, length, 3 * pair),
            vmem(pairs, length, 3 * pair),
        ]
    scratch = [
        vmem(width, 4 * width),
        vmem(width, width),
        vmem(length, 4 * width),
        pltpu.VMEM((length, 4 * width), F32),
        vmem(pairs, 2 * length, length),
        pltpu.VMEM((pairs, 2 * length, length), F32),
        *exchanged,
        vmem(length, width),
        vmem(length, width),
        pltpu.SMEM((1, plan.shards), jnp.int32),
        pltpu.SMEM((1, plan.shards // 2), jnp.int32),
        vmem(1, length, width),
        vmem(1, length, width),
        pltpu.SemaphoreType.DMA((9,)),
        pltpu.SemaphoreType.DMA((plan.copies(),)),
        pltpu.SemaphoreType.DMA((plan.copies(),)),
    ]
    for spec in plan.chunks:
        scratch += [vmem(*shape) for shape in plan.scratch_of(*spec)]
    for name in PARTS if quad else ():
        scratch += [vmem(*shape) for shape in plan.part_scratch(name)]
    in_vmem = pl.BlockSpec(memory_space=pltpu.VMEM)
    in_hbm = pl.BlockSpec(memory_space=pltpu.HBM)
    results = pl.pallas_call(
        functools.partial(quad_kernel if quad else kernel, plan, scale),
        out_shape=(
            pltpu.VMEM(sequences.shape, BF16),
            pltpu.VMEM(sequences.shape, BF16),
            pltpu.VMEM((plan.share, 4 * width), F32),
            pltpu.VMEM((plan.share, width), F32),
        ),
        in_specs=[in_hbm] * 6,
        out_specs=(in_vmem,) * 4,
        scratch_shapes=scratch,
        compiler_params=pltpu.CompilerParams(
            collective_id=0, has_side_effects=True, vmem_limit_bytes=LIMIT
        ),
    )(lengths[:, :, 0], swap_table[:, :, 0], sequences, upstream, input_weight, output_weight)
    return pl.pallas_call(
        store_kernel,
        out_shape=tuple(jax.ShapeDtypeStruct(r.shape, r.dtype) for r in results),
        in_specs=[pl.BlockSpec(memory_space=pl.ANY)] * 4,
        out_specs=(in_hbm,) * 4,
        scratch_shapes=[pltpu.SemaphoreType.DMA((4,))],
        compiler_params=pltpu.CompilerParams(vmem_limit_bytes=8 * 1024 * 1024),
    )(*results)


def solution(mesh):
    groups, shards = mesh.shape["grp"], mesh.shape["wide"]
    split = P(("grp", "wide"), None, None)

    def whole(sequences, upstream, lengths, swap_table, input_weight, output_weight):
        sizes = groups, shards, sequences.shape[1], sequences.shape[2]
        plan = QuadPlan(*sizes) if QuadPlan.fits(*sizes) else Plan(*sizes)
        return jax.shard_map(
            functools.partial(body, plan),
            mesh=mesh,
            in_specs=(split, split, P("grp", None, None), P("grp", None, None), P(), P()),
            out_specs=(split, split, P("wide", None), P("wide", None)),
            check_vma=False,
        )(sequences, upstream, lengths, swap_table, input_weight, output_weight)

    return whole
```
